32 devices in a mesh: dp: 8 (over z, x), mp: 4 (over y, core).
Axes of the slice: x: 2, y: 2, z: 4, core: 2. Of those that a mesh axis runs over, the one named last changes fastest.
Arguments:
- tokens: bfloat16 [32, 512, 768], P('dp'), may hold values from -6 to 6
- visible: int32 [32], P('dp'), may hold values from 129 to 512, as said below
- w_query: bfloat16 [768, 768], P(None, 'mp'), may hold values from -0.21875 to 0.21875
- b_query: bfloat16 [768], P('mp'), may hold values from -3 to 3
- w_key: bfloat16 [768, 768], P(None, 'mp'), may hold values from -0.21875 to 0.21875
- w_value: bfloat16 [768, 768], P(None, 'mp'), may hold values from -0.21875 to 0.21875
- b_value: bfloat16 [768], P('mp'), may hold values from -3 to 3
- w_output: bfloat16 [768, 768], P('mp'), may hold values from -1.75 to 1.75
- b_output: bfloat16 [768], replicated, may hold values from -2 to 2
- w_expand: bfloat16 [768, 3072], P(None, 'mp'), may hold values from -0.21875 to 0.21875
- b_expand: bfloat16 [3072], P('mp'), may hold values from -3 to 3
- w_reduce: bfloat16 [3072, 768], P('mp'), may hold values from -0.21875 to 0.21875
- b_reduce: bfloat16 [768], replicated, may hold values from -2 to 2
- gain_first: bfloat16 [768], replicated, may hold values from 0.5 to 1.5
- shift_first: bfloat16 [768], replicated, may hold values from -2 to 2
- gain_second: bfloat16 [768], replicated, may hold values from 0.5 to 1.5
- shift_second: bfloat16 [768], replicated, may hold values from -2 to 2
- cotangent: bfloat16 [32, 512, 768], P('dp'), may hold values from -6 to 6
Outputs:
- result: bfloat16 [32, 512, 768], P('dp')
- grad_tokens: bfloat16 [32, 512, 768], P('dp')
- grad_query: float32 [768, 768], P('dp', 'mp')
- grad_bquery: float32 [768], P('mp')
- grad_key: float32 [768, 768], P('dp', 'mp')
- grad_value: float32 [768, 768], P('dp', 'mp')
- grad_bvalue: float32 [768], P('mp')
- grad_output: float32 [768, 768], P('mp', 'dp')
- grad_boutput: float32 [768], replicated
- grad_expand: float32 [768, 3072], P('dp', 'mp')
- grad_bexpand: float32 [3072], P('mp')
- grad_reduce: float32 [3072, 768], P('mp', 'dp')
- grad_breduce: float32 [768], replicated
- grad_gain_first: float32 [768], replicated
- grad_shift_first: float32 [768], replicated
- grad_gain_second: float32 [768], replicated
- grad_shift_second: float32 [768], replicated
The draws below stay inside these ranges and needn't reach their ends.
Inputs may be any that keep to these rules, and one draw needn't show every extreme that they name: Number of visible patches of each strip, the other of its 512 slots being padding; in every aligned block of 4 strips one strip has all 512 slots visible.
All inputs are finite; a program needn't handle non-finite values.
Results may differ from the reference program's by a relative error of at most 0.018.
Values may be sent and summed in bfloat16 or wider, within the bound.
No kernel may reach another device: no remote copies, remote signals or barrier semaphores. Data moves between devices by JAX's collectives and lax.ppermute only.
A program may use at most 192 MiB of HBM per device.

```python
import math
import jax
import jax.numpy as jnp
from jax import lax

D = 768
H = 12
HD = 64
FF = 3072
VIS = 512
STRIP_DEV = 4
STRIPS = 32
N_MP = 4


def draw_visible(key, part):
    first_key, second_key, third_key = jax.random.split(key, 3)
    drop_first = jax.random.randint(first_key, (STRIPS,), 0, 3 * VIS // 4)
    drop_second = jax.random.randint(second_key, (STRIPS,), 0, 3 * VIS // 4)
    dropped = jnp.minimum(drop_first, drop_second)
    full_slot = jax.random.randint(third_key, (STRIPS // STRIP_DEV,), 0, STRIP_DEV)
    position = jnp.arange(STRIPS, dtype=jnp.int32) % STRIP_DEV
    is_full = position == jnp.repeat(full_slot, STRIP_DEV)
    return jnp.where(is_full, VIS, VIS - dropped).astype(jnp.int32)


def spiked(entries, stream_key, source, target, blocks, factor):
    owner, partner = [(jnp.arange(entries.shape[dim]) // (entries.shape[dim] // blocks)).reshape([-1 if axis == dim else 1 for axis in range(entries.ndim)]) for dim in (source, target)]
    chosen = jax.random.permutation(stream_key, blocks)[partner]
    strong = (owner == chosen) | (owner == (partner + blocks // 2) % blocks)
    return jnp.where(strong, factor * entries, entries)


def steps_of(rng, extent, cuts, low, largest):
    loudness, own = 1.0, jax.random.fold_in(rng, 6)
    for axis_at, parts in cuts:
        heights = jnp.exp(jax.random.uniform(jax.random.fold_in(own, axis_at), (parts,), jnp.float32, low / len(cuts), largest / len(cuts)))
        loudness = loudness * jnp.repeat(heights, extent[axis_at] // parts).reshape([-1 if axis == axis_at else 1 for axis in range(len(extent))])
    return loudness


def centred(own_key, extent, scale, reach, shards=(), kind=jnp.bfloat16):
    result = jax.random.normal(own_key, extent, jnp.float32) * scale
    if len(shards) > 0:
        result = steps_of(own_key, extent, shards, -0.22, 0.18) * result
    return jnp.clip(result, min=-reach, max=reach).astype(kind)


def heavy_noise(stream_key, shape, scale, limit, shards, heavy, held_as=jnp.bfloat16):
    drawn = scale * jax.random.normal(stream_key, shape, jnp.float32)
    if shards:
        drawn = drawn * steps_of(stream_key, shape, shards, -0.22, 0.18)
    return jnp.clip(spiked(drawn, jax.random.fold_in(stream_key, 3), *heavy), -limit, limit).astype(held_as)


def setup_inputs(seed: int = 0) -> dict:
    key_list = jax.random.split(jax.random.key(seed), 19)
    return {
        "tokens": heavy_noise(key_list[0], (STRIPS, VIS, D), 1.0, 6.0, ((0, 8),), (0, 2, 8, 2.0)),
        "visible": draw_visible(jax.random.fold_in(key_list[18], 71), 0),
        "w_query": centred(key_list[2], (D, D), D ** -0.5, 0.21875, ((1, 4),)),
        "b_query": centred(key_list[3], (D,), 0.5, 3.0, ((0, 4),)),
        "w_key": centred(key_list[4], (D, D), D ** -0.5, 0.21875, ((1, 4),)),
        "w_value": centred(key_list[5], (D, D), D ** -0.5, 0.21875, ((1, 4),)),
        "b_value": centred(key_list[6], (D,), 0.5, 3.0, ((0, 4),)),
        "w_output": centred(key_list[7], (D, D), (D // 64) ** -0.5, 1.75, ((0, 4),)),
        "b_output": centred(key_list[8], (D,), 0.3, 2.0),
        "w_expand": centred(key_list[9], (D, FF), D ** -0.5, 0.21875, ((1, 4),)),
        "b_expand": centred(key_list[10], (FF,), 0.5, 3.0, ((0, 4),)),
        "w_reduce": centred(key_list[11], (FF, D), (FF // 4) ** -0.5, 0.21875, ((0, 4),)),
        "b_reduce": centred(key_list[12], (D,), 0.3, 2.0),
        "gain_first": jnp.clip(1.0 + 0.1 * jax.random.normal(key_list[13], (D,), jnp.float32), 0.5, 1.5).astype(jnp.bfloat16),
        "shift_first": centred(key_list[14], (D,), 0.3, 2.0),
        "gain_second": jnp.clip(1.0 + 0.1 * jax.random.normal(key_list[15], (D,), jnp.float32), 0.5, 1.5).astype(jnp.bfloat16),
        "shift_second": centred(key_list[16], (D,), 0.3, 2.0),
        "cotangent": heavy_noise(key_list[17], (STRIPS, VIS, D), 1.0, 6.0, ((0, 8),), (0, 2, 8, 2.0)),
    }


@jax.custom_vjp
def low(v):
    return lax.optimization_barrier(v.astype(jnp.bfloat16)).astype(jnp.float32)

@jax.custom_vjp
def low_back(v):
    return v

def low_keep(v):
    return (low(v), None)

def low_pass(kept, grad):
    return (grad,)

def back_keep(v):
    return (v, None)

def back_low(kept, grad):
    return (low(grad),)
low.defvjp(low_keep, low_pass)
low_back.defvjp(back_keep, back_low)

def multiply(form, left, right):
    return jnp.einsum(form, left, right, precision=lax.Precision.HIGHEST)

def layer_norm(values, gain, shift):
    center = values - lax.optimization_barrier(jnp.mean(values, axis=-1, keepdims=True))
    spread = lax.optimization_barrier(jnp.mean(center * center, axis=-1, keepdims=True))
    return center * lax.rsqrt(spread + 1e-06) * gain + shift

def forward(source, params, valid):
    w_query, b_query, w_key, w_value, b_value, w_output, b_output, w_expand, b_expand, w_reduce, b_reduce, gain_first, shift_first, gain_second, shift_second = params
    group, slots = (source.shape[0], source.shape[1])
    normed = low(layer_norm(source, gain_first, shift_first))
    queries = low(low_back(multiply('svd,de->sve', normed, w_query) + b_query)).reshape(group, slots, H, HD)
    keysp = low(low_back(multiply('svd,de->sve', normed, w_key))).reshape(group, slots, H, HD)
    values = low(low_back(multiply('svd,de->sve', normed, w_value) + b_value)).reshape(group, slots, H, HD)
    scores = low_back(multiply('sqhd,skhd->shqk', queries, keysp) * HD ** (-0.5))
    scores = jnp.where(valid[:, None, None, :], scores, -1e+30)
    probs = jax.nn.softmax(scores, axis=-1)
    context = low(low_back(multiply('shqk,skhd->sqhd', low(probs), values)))
    context = context.reshape(group, slots, N_MP, D // N_MP)
    partial_attn = multiply('sqgc,gcd->sqgd', context, w_output.reshape(N_MP, D // N_MP, D))
    attn = low_back(lax.optimization_barrier(jnp.sum(low(partial_attn), axis=2)) + b_output)
    resid = source + attn
    normed_two = low(layer_norm(resid, gain_second, shift_second))
    pre_act = low_back(multiply('svd,df->svf', normed_two, w_expand) + b_expand)
    hidden = low(jax.nn.gelu(pre_act, approximate=False)).reshape(group, slots, N_MP, FF // N_MP)
    partial_mlp = multiply('sqgf,gfd->sqgd', hidden, w_reduce.reshape(N_MP, FF // N_MP, D))
    mlp = low_back(lax.optimization_barrier(jnp.sum(low(partial_mlp), axis=2)) + b_reduce)
    return valid.astype(jnp.float32)[:, :, None] * (resid + mlp)

def reference(tokens, visible, w_query, b_query, w_key, w_value, b_value, w_output, b_output, w_expand, b_expand, w_reduce, b_reduce, gain_first, shift_first, gain_second, shift_second, cotangent):
    params = tuple((item.astype(jnp.float32) for item in (w_query, b_query, w_key, w_value, b_value, w_output, b_output, w_expand, b_expand, w_reduce, b_reduce, gain_first, shift_first, gain_second, shift_second)))
    group = math.gcd(STRIPS, 8)
    blocks = STRIPS // group
    sources = tokens.astype(jnp.float32).reshape(blocks, group, VIS, D)
    upstream = cotangent.astype(jnp.float32).reshape(blocks, group, VIS, D)
    valid = jnp.arange(VIS, dtype=jnp.int32)[None, :] < visible[:, None]
    valid = valid.reshape(blocks, group, VIS)

    def step(totals, item):
        source, incoming, mask = item

        def run(src, weights):
            return forward(src, weights, mask)
        output, pull = jax.vjp(run, source, params)
        d_source, d_params = pull(incoming)
        totals = jax.tree.map(lambda first, second: first + second, totals, d_params)
        return (totals, (output.astype(jnp.bfloat16), d_source.astype(jnp.bfloat16)))
    zeros = jax.tree.map(jnp.zeros_like, params)
    totals, (outputs, d_tokens) = lax.scan(step, zeros, (sources, upstream, valid))
    outputs = outputs.reshape(STRIPS, VIS, D)
    d_tokens = d_tokens.reshape(STRIPS, VIS, D)
    return (outputs, d_tokens) + tuple(totals)
```

```python
from functools import partial

import jax
import jax.numpy as jnp
from jax import lax
from jax.experimental import pallas as pl
from jax.experimental.pallas import tpu as pltpu
from jax.sharding import PartitionSpec as P

HD = 64
F32 = jnp.float32
BF = jnp.bfloat16
NT = (((1,), (1,)), ((), ()))
VMEM = pl.BlockSpec(memory_space=pltpu.VMEM)
SMEM = pl.BlockSpec(memory_space=pltpu.SMEM)


def dot(left, right):
    return jnp.dot(left, right, preferred_element_type=F32)


def dot_nt(left, right):
    return lax.dot_general(left, right, NT, preferred_element_type=F32)


def shape(dims, dtype):
    return jax.ShapeDtypeStruct(dims, dtype)


def call(body, outs, args, flops, limit=48, scratch=()):
    specs = [SMEM if a.dtype == jnp.int32 else VMEM for a in args]
    moved = sum(a.size * a.dtype.itemsize for a in list(args) + list(outs))
    return pl.pallas_call(
        body,
        in_specs=specs,
        out_shape=tuple(outs),
        scratch_shapes=list(scratch),
        cost_estimate=pl.CostEstimate(flops=flops, bytes_accessed=moved, transcendentals=0),
        compiler_params=pltpu.CompilerParams(vmem_limit_bytes=limit << 20),
    )(*args)


def norm_parts(values):
    center = values - jnp.mean(values, axis=-1, keepdims=True)
    rstd = lax.rsqrt(jnp.mean(center * center, axis=-1, keepdims=True) + 1e-06)
    return center * rstd, rstd


def norm_back(unit, rstd, gain, grad):
    scaled = grad * gain
    first = jnp.mean(scaled, axis=-1, keepdims=True)
    second = jnp.mean(scaled * unit, axis=-1, keepdims=True)
    return rstd * (scaled - first - unit * second)


def row_sum(values):
    return jnp.sum(values, axis=0, keepdims=True)


def norm_one_body(tok, gain, shift, normed, normed_t):
    unit, _ = norm_parts(tok[...].astype(F32))
    low = (unit * gain[...].astype(F32) + shift[...].astype(F32)).astype(BF)
    normed[...] = low
    normed_t[...] = low.T


def norm_one(tok, gain, shift):
    rows, width = tok.shape
    outs = (shape((rows, width), BF), shape((width, rows), BF))
    return call(norm_one_body, outs, (tok, gain, shift), 10 * rows * width)


def attn_fwd_body(slots, visible, normed, *refs):
    wq, wk, wv = refs[:slots], refs[slots : 2 * slots], refs[2 * slots : 3 * slots]
    small = refs[3 * slots : 4 * slots]
    q_out, k_out, v_out, e_out, o_out, ctx_out = refs[4 * slots :]
    rows, _ = normed.shape
    part = wq[0].shape[1]
    heads = part // HD
    lane = lax.broadcasted_iota(jnp.int32, (rows, HD), 1)
    row = lax.broadcasted_iota(jnp.int32, (rows, HD), 0)
    one = jnp.where(lane == 0, 1.0, 0.0).astype(BF)
    mask = jnp.where((lane == 0) & (row >= visible[0]), -1e30, 0.0).astype(BF)
    low = normed[...]
    for s in range(slots):
        q = ((dot(low, wq[s][...]) + small[s][1:2, :part].astype(F32)).astype(BF) * BF(HD**-0.5))
        k = dot(low, wk[s][...]).astype(BF)
        v = (dot(low, wv[s][...]) + small[s][1:2, part : 2 * part].astype(F32)).astype(BF)
        for h in range(heads):
            cols = slice(h * HD, (h + 1) * HD)
            i = s * heads + h
            q_out[i, :, :HD] = q[:, cols]
            q_out[i, :, HD:] = one
            k_out[i, :, :HD] = k[:, cols]
            k_out[i, :, HD:] = mask
            v_out[i, :, :HD] = v[:, cols]
            v_out[i, :, HD:] = one
    for i in range(slots * heads):
        scores = dot_nt(q_out[i], k_out[i])
        e = jnp.exp(scores - jnp.max(scores, axis=1, keepdims=True)).astype(BF)
        e_out[i] = e
        o = dot(e, v_out[i])
        o_out[i] = o
        ctx_out[:, i * HD : (i + 1) * HD] = (o[:, :HD] * (1.0 / o[:, HD : HD + 1])).astype(BF)


def attn_fwd(visible, normed, wq, wk, wv, small):
    slots = len(wq)
    rows, width = normed.shape
    part = wq[0].shape[1]
    n = slots * part // HD
    outs = [shape((n, rows, 2 * HD), BF)] * 3
    outs += [shape((n, rows, rows), BF), shape((n, rows, 2 * HD), F32), shape((rows, n * HD), BF)]
    flops = 2 * rows * width * 3 * slots * part + 2 * n * 2 * rows * rows * HD
    return call(partial(attn_fwd_body, slots), outs, (visible, normed, *wq, *wk, *wv, *small), flops)


def middle_body(pairs, visible, tok, cot, bias, gain, shift, *refs):
    ctx, wo = refs[:pairs], refs[pairs : pairs + 2 * pairs]
    resid, normed, normed_t, branch, branch_t, d_bias = refs[3 * pairs :]
    rows, _ = tok.shape
    part = wo[0].shape[0]
    total = tok[...].astype(F32) + bias[...].astype(F32)
    for p in range(pairs):
        for s in range(2):
            total += dot(ctx[p][:, s * part : (s + 1) * part], wo[2 * p + s][...])
    resid[...] = total
    unit, _ = norm_parts(total)
    low = (unit * gain[...].astype(F32) + shift[...].astype(F32)).astype(BF)
    normed[...] = low
    normed_t[...] = low.T
    row = lax.broadcasted_iota(jnp.int32, cot.shape, 0)
    kept = jnp.where(row < visible[0], cot[...].astype(F32), 0.0)
    branch[...] = kept.astype(BF)
    branch_t[...] = kept.astype(BF).T
    d_bias[...] = row_sum(kept)


def middle(visible, tok, cot, bias, gain, shift, ctx, wo):
    rows, width = tok.shape
    flat, tall = shape((rows, width), BF), shape((width, rows), BF)
    outs = (shape((rows, width), F32), flat, tall, flat, tall, shape((1, width), F32))
    args = (visible, tok, cot, bias, gain, shift, *ctx, *wo)
    return call(partial(middle_body, len(ctx)), outs, args, 2 * rows * width * width)


def ffn_body(slots, carried, normed, normed_t, branch, branch_t, *refs):
    we, wr, small = refs[:slots], refs[slots : 2 * slots], refs[2 * slots : 3 * slots]
    refs = refs[3 * slots :]
    carry, refs = refs[: 2 * carried], refs[2 * carried :]
    grads, d_small, mlp, d_norm = refs[:slots], refs[slots], refs[slots + 1], refs[slots + 2]
    units = we[0].shape[1]
    for s in range(slots):
        pre = dot(normed[...], we[s][...]) + small[s][0:1, :].astype(F32)
        cdf = 0.5 * (1.0 + lax.erf(pre * 0.7071067811865476))
        slope = cdf + pre * (jnp.exp(-0.5 * pre * pre) * 0.3989422804014327)
        hidden = (pre * cdf).astype(BF)
        d_pre = (dot_nt(branch[...], wr[s][...]) * slope).astype(BF)
        d_small[s : s + 1, :] = row_sum(d_pre.astype(F32))
        out = dot(hidden, wr[s][...])
        back = dot_nt(d_pre, we[s][...])
        if s == 0 and not carried:
            mlp[...] = out
            d_norm[...] = back
        elif s == 0:
            mlp[...] = carry[0][...] + out
            d_norm[...] = carry[1][...] + back
        else:
            mlp[...] += out
            d_norm[...] += back
        grads[s][:, :units] = dot(normed_t[...], d_pre).astype(BF)
        grads[s][:, units:] = dot(branch_t[...], hidden).astype(BF)


def ffn(normed, normed_t, branch, branch_t, we, wr, small, carry=()):
    slots = len(we)
    rows, width = normed.shape
    units = we[0].shape[1]
    outs = [shape((width, 2 * units), BF)] * slots + [shape((8, units), F32)] + [shape((rows, width), F32)] * 2
    args = (normed, normed_t, branch, branch_t, *we, *wr, *small, *carry)
    return call(partial(ffn_body, slots, len(carry) // 2), outs, args, 12 * rows * width * units * slots)


def turn_body(visible, resid, mlp, bias, d_norm, branch, gain, result, grad, attn, attn_t, sums):
    row = lax.broadcasted_iota(jnp.int32, resid.shape, 0)
    base = resid[...]
    total = base + (mlp[...] + bias[...].astype(F32))
    result[...] = jnp.where(row < visible[0], total, 0.0).astype(BF)
    unit, rstd = norm_parts(base)
    dn = d_norm[...]
    g = branch[...].astype(F32) + norm_back(unit, rstd, gain[...].astype(F32), dn)
    grad[...] = g
    low = g.astype(BF)
    attn[...] = low
    attn_t[...] = low.T
    sums[0:1, :] = row_sum(low.astype(F32))
    sums[1:2, :] = row_sum(dn * unit)
    sums[2:3, :] = row_sum(dn)


def turn(visible, resid, mlp, bias, d_norm, branch, gain):
    rows, width = resid.shape
    outs = (shape((rows, width), BF), shape((rows, width), F32), shape((rows, width), BF))
    outs += (shape((width, rows), BF), shape((8, width), F32))
    return call(turn_body, outs, (visible, resid, mlp, bias, d_norm, branch, gain), 30 * rows * width)


def attn_bwd_body(slots, carried, attn, attn_t, normed_t, q_in, k_in, v_in, e_in, o_in, ctx, *refs):
    wo, wq, wk, wv = (refs[i * slots : (i + 1) * slots] for i in range(4))
    refs = refs[4 * slots :]
    carry, refs = refs[:carried], refs[carried:]
    grads, d_small, d_norm = refs[:slots], refs[slots], refs[slots + 1]
    d_in = refs[slots + 2]
    rows, _ = attn.shape
    part = wq[0].shape[1]
    heads = part // HD
    lane = lax.broadcasted_iota(jnp.int32, (rows, HD), 1)
    for s in range(slots):
        d_ctx = dot_nt(attn[...], wo[s][...]).astype(BF).astype(F32)
        back_v, back_k = [], []
        for h in range(heads):
            i = s * heads + h
            o = o_in[i]
            inverse = 1.0 / o[:, HD : HD + 1]
            do = (d_ctx[:, h * HD : (h + 1) * HD] * inverse).astype(BF)
            term = jnp.sum(do.astype(F32) * o[:, :HD], axis=1, keepdims=True) * inverse
            e = e_in[i]
            d_prob = dot_nt(do, v_in[i][:, :HD])
            d_score = (e.astype(F32) * (d_prob - term)).astype(BF)
            back_v.append(dot(do.T, e))
            back_k.append(dot(q_in[i][:, :HD].T, d_score))
            d_in[:, h * HD : (h + 1) * HD] = (dot(d_score, k_in[i][:, :HD]) * HD**-0.5).astype(BF)
        d_in[:, part : 2 * part] = jnp.concatenate(back_k, axis=0).T.astype(BF)
        d_in[:, 2 * part : 3 * part] = jnp.concatenate(back_v, axis=0).T.astype(BF)
        dq, dk, dv = (d_in[:, i * part : (i + 1) * part] for i in range(3))
        d_small[s : s + 1, :part] = row_sum(dq.astype(F32))
        d_small[s : s + 1, part : 2 * part] = row_sum(dv.astype(F32))
        back = dot_nt(dq, wq[s][...]) + dot_nt(dk, wk[s][...]) + dot_nt(dv, wv[s][...])
        if s == 0 and not carried:
            d_norm[...] = back
        elif s == 0:
            d_norm[...] = carry[0][...] + back
        else:
            d_norm[...] += back
        grads[s][:, : 3 * part] = dot(normed_t[...], d_in[...]).astype(BF)
        grads[s][:, 3 * part :] = dot(attn_t[...], ctx[:, s * part : (s + 1) * part]).astype(BF)


def attn_bwd(attn, attn_t, normed_t, saved, wo, wq, wk, wv, carry=()):
    slots = len(wq)
    rows, width = attn.shape
    part = wq[0].shape[1]
    outs = [shape((width, 4 * part), BF)] * slots + [shape((8, width), F32), shape((rows, width), F32)]
    args = (attn, attn_t, normed_t, *saved, *wo, *wq, *wk, *wv, *carry)
    flops = slots * part * (16 * rows * width + 10 * rows * rows)
    scratch = (pltpu.VMEM((rows, 3 * part), BF),)
    return call(partial(attn_bwd_body, slots, len(carry)), outs, args, flops, 50, scratch)


def norm_one_back_body(tok, gain, d_norm, grad, out, sums):
    unit, rstd = norm_parts(tok[...].astype(F32))
    dn = d_norm[...]
    out[...] = (grad[...] + norm_back(unit, rstd, gain[...].astype(F32), dn)).astype(BF)
    sums[0:1, :] = row_sum(dn * unit)
    sums[1:2, :] = row_sum(dn)


def norm_one_back(tok, gain, d_norm, grad):
    rows, width = tok.shape
    outs = (shape((rows, width), BF), shape((8, width), F32))
    return call(norm_one_back_body, outs, (tok, gain, d_norm, grad), 20 * rows * width)


def swap(values, axis, size, bit):
    return lax.ppermute(values, axis, [(i, i ^ (1 << bit)) for i in range(size)])


def pick(values, index, axis):
    return lax.dynamic_index_in_dim(values, index, axis, keepdims=False)


def scatter_sum(values, size, index):
    width = values.shape[-1]
    block = values.shape[-2] // size
    lead = values.shape[:-2]
    for bit in range(size.bit_length() - 1):
        size_now = size >> bit
        split = values.reshape(*lead, size_now // 2, 2, block, width)
        mine = (index >> bit) & 1
        away = pick(split, 1 - mine, len(lead) + 1)
        kept = pick(split, mine, len(lead) + 1)
        got = swap(away, "dp", size, bit)
        values = (kept.astype(F32) + got.astype(F32)).astype(values.dtype)
    return values.reshape(*lead, block, width)


def spread_body(index, *refs):
    ins, out, sem = refs[:4], refs[4], refs[5]
    copies = [pltpu.make_async_copy(ins[s], out.at[index[0] ^ s], sem.at[s]) for s in range(4)]
    for copy in copies:
        copy.start()
    for copy in copies:
        copy.wait()


def spread(index, strips):
    rows, width = strips[0].shape
    return pl.pallas_call(
        spread_body,
        in_specs=[SMEM] + [pl.BlockSpec(memory_space=pl.ANY)] * 4,
        out_specs=pl.BlockSpec(memory_space=pl.ANY),
        out_shape=shape((4, rows, width), strips[0].dtype),
        scratch_shapes=[pltpu.SemaphoreType.DMA((4,))],
    )(index, *strips)


def local(
    sizes,
    tokens,
    visible,
    w_query,
    b_query,
    w_key,
    w_value,
    b_value,
    w_output,
    b_output,
    w_expand,
    b_expand,
    w_reduce,
    b_reduce,
    gain_first,
    shift_first,
    gain_second,
    shift_second,
    cotangent,
):
    n_dp, n_mp = sizes
    dp, mp = lax.axis_index("dp"), lax.axis_index("mp")
    part, units, width = w_query.shape[1], w_expand.shape[1], tokens.shape[2]
    core = partial(swap, axis="mp", size=n_mp, bit=0)
    across = partial(swap, axis="mp", size=n_mp, bit=1)

    def gather(own):
        near, far = core(own), across(own)
        return [own, near, far, core(far)]

    def flat(vector):
        return vector.reshape(1, -1)

    tok, cot = pick(tokens, mp, 0), pick(cotangent, mp, 0)
    vis = pick(visible, mp, 0).reshape(1)
    small_own = jnp.zeros((16, units), BF)
    small_own = small_own.at[0].set(b_expand)
    small_own = small_own.at[1, :part].set(b_query).at[1, part : 2 * part].set(b_value)
    small = gather(small_own)
    wq, wk, wv = gather(w_query), gather(w_key), gather(w_value)
    wo = gather(w_output)
    we, wr = gather(w_expand), gather(w_reduce)

    n1, n1t = norm_one(tok, flat(gain_first), flat(shift_first))
    near = attn_fwd(vis, n1, wq[:2], wk[:2], wv[:2], small[:2])
    away = attn_fwd(vis, n1, wq[2:], wk[2:], wv[2:], small[2:])
    resid, n2, n2t, branch, branch_t, d_reduce = middle(
        vis, tok, cot, flat(b_output), flat(gain_second), flat(shift_second), (near[5], away[5]), wo
    )
    g0, g1, de_near, mlp, dn2 = ffn(n2, n2t, branch, branch_t, we[:2], wr[:2], small[:2])
    got0 = core(g1)
    g2, g3, de_away, mlp, dn2 = ffn(
        n2, n2t, branch, branch_t, we[2:], wr[2:], small[2:], (mlp, dn2)
    )
    got2 = core(g3)
    strip, grad_resid, attn, attn_t, sums2 = turn(
        vis, resid, mlp, flat(b_reduce), dn2, branch, flat(gain_second)
    )
    result = spread(mp.reshape(1), gather(strip))

    def add(left, right):
        return (left.astype(F32) + right.astype(F32)).astype(BF)

    def finish(left, right):
        return left.astype(F32) + right.astype(F32)

    expand_sum = add(add(g0[:, :units], got0[:, :units]), across(add(g2[:, :units], got2[:, :units])))
    grad_expand = scatter_sum(expand_sum, n_dp, dp).astype(F32)
    reduce_sum = jnp.stack([add(g0[:, units:], got0[:, units:]), add(g2[:, units:], got2[:, units:])])
    reduce_sum = scatter_sum(reduce_sum, n_dp, dp)
    grad_reduce = finish(reduce_sum[0], across(reduce_sum[1])).T

    h2, h3, ds_away, dn1 = attn_bwd(attn, attn_t, n1t, away, wo[2:], wq[2:], wk[2:], wv[2:])
    sum2 = scatter_sum(add(h2, core(h3)), n_dp, dp)
    h0, h1, ds_near, dn1 = attn_bwd(attn, attn_t, n1t, near, wo[:2], wq[:2], wk[:2], wv[:2], (dn1,))
    sum0 = scatter_sum(add(h0, core(h1)), n_dp, dp)
    heads_sum = finish(sum0, across(sum2))
    grad_query, grad_key = heads_sum[:, :part], heads_sum[:, part : 2 * part]
    grad_value, grad_output = heads_sum[:, 2 * part : 3 * part], heads_sum[:, 3 * part :].T
    grad_strip, sums1 = norm_one_back(tok, flat(gain_first), dn1, grad_resid)
    grad_tokens = spread(mp.reshape(1), gather(grad_strip))

    slots = [jnp.stack([e, s]) for e, s in zip([*de_near[:2], *de_away[:2]], [*ds_near[:2], *ds_away[:2]])]
    shared = jnp.concatenate([d_reduce, sums2[:3], sums1[:2]])
    got = core(jnp.concatenate([slots[1], slots[3], shared]))
    slots0, slots2, shared = slots[0] + got[:2], slots[2] + got[2:4], shared + got[4:]
    got = across(jnp.concatenate([slots2, shared]))
    totals = jnp.concatenate([slots0, shared]) + got
    for bit in range(n_dp.bit_length() - 1):
        totals = totals + swap(totals, "dp", n_dp, bit)
    return (
        result,
        grad_tokens,
        grad_query,
        totals[1, :part],
        grad_key,
        grad_value,
        totals[1, part : 2 * part],
        grad_output,
        totals[3],
        grad_expand,
        totals[0],
        grad_reduce,
        totals[2],
        totals[6],
        totals[7],
        totals[4],
        totals[5],
    )


def solution(mesh):
    placed = (
        P("dp", None, None),
        P("dp"),
        P(None, "mp"),
        P("mp"),
        P(None, "mp"),
        P(None, "mp"),
        P("mp"),
        P("mp", None),
        P(),
        P(None, "mp"),
        P("mp"),
        P("mp", None),
        P(),
        P(),
        P(),
        P(),
        P(),
        P("dp", None, None),
    )
    return jax.shard_map(
        partial(local, (mesh.shape["dp"], mesh.shape["mp"])),
        mesh=mesh,
        in_specs=placed,
        out_specs=(
            P("dp", None, None),
            P("dp", None, None),
            P("dp", "mp"),
            P("mp"),
            P("dp", "mp"),
            P("dp", "mp"),
            P("mp"),
            P("mp", "dp"),
            P(),
            P("dp", "mp"),
            P("mp"),
            P("mp", "dp"),
            P(),
            P(),
            P(),
            P(),
            P(),
        ),
        check_vma=False,
    )
```

```python
from functools import partial

import jax
import jax.numpy as jnp
from jax import lax
from jax.experimental import pallas as pl
from jax.experimental.pallas import tpu as pltpu
from jax.sharding import PartitionSpec as P

HD = 64
F32 = jnp.float32
BF = jnp.bfloat16
NT = (((1,), (1,)), ((), ()))
ANY = pl.BlockSpec(memory_space=pl.ANY)
SMEM = pl.BlockSpec(memory_space=pltpu.SMEM)
VMEM = pl.BlockSpec(memory_space=pltpu.VMEM)


def dot(left, right):
    return jnp.dot(left, right, preferred_element_type=F32)


def dot_nt(left, right):
    return lax.dot_general(left, right, NT, preferred_element_type=F32)


def shape(dims, dtype):
    return jax.ShapeDtypeStruct(dims, dtype)


class Load:
    def __init__(self, buffer, copies=()):
        self.buffer, self.copies = buffer, copies
        for copy in copies:
            copy.start()

    def ref(self):
        for copy in self.copies:
            copy.wait()
        self.copies = ()
        return self.buffer

    def __getitem__(self, index):
        return self.ref()[index]

    @property
    def shape(self):
        return self.buffer.shape


class Store:
    def __init__(self, buffer, target=None, sems=None):
        self.target, self.buffer, self.sems = target, buffer, sems
        self.copies = []

    def start(self, source, target):
        self.copies.append(pltpu.make_async_copy(source, target, self.sems.at[len(self.copies)]))
        self.copies[-1].start()

    def send(self, *index):
        if self.target is not None:
            self.start(*((self.buffer.at[index], self.target.at[index]) if index else (self.buffer, self.target)))

    def send_from(self, view):
        self.start(view, self.target)

    def close(self):
        if not self.copies:
            self.send()
        for copy in self.copies:
            copy.wait()

    def __setitem__(self, index, value):
        self.buffer[index] = value

    def __getitem__(self, index):
        return self.buffer[index]

    @property
    def shape(self):
        return self.buffer.shape


class Held:
    def __init__(self, dims, dtype):
        self.struct = shape(dims, dtype)


PIECES = 8
SMALL = 16


class Arg:
    def __init__(self, arrays, dims, view=None, offset=None, counts=None, held=False):
        self.arrays, self.dims, self.view, self.offset, self.held = arrays, dims, view, offset, held
        self.counts = counts or [a.shape[0] for a in arrays]


def own(array):
    return Arg([array], array.shape[1:], view=lambda ref, here: ref.at[here["strip"]])


def other(array):
    return Arg([array], array.shape[1:], view=lambda ref, here: ref.at[here["strip"] ^ 2])


def entry(array, index):
    return Arg([array], array.shape[1:], view=lambda ref, here: ref.at[index])


def held(array, first=None, count=None):
    if first is None:
        return Arg([array], array.shape, held=True)
    view = lambda ref, here: ref.at[pl.ds(first, count)]
    return Arg([array], (count, *array.shape[1:]), view=view, held=True)


def rows_of(array, first, count):
    return Arg([array], (count, *array.shape[1:]), view=lambda ref, here: ref.at[pl.ds(first, count)])


def stacked(*arrays, counts=None):
    counts = counts or [a.shape[0] for a in arrays]
    starts = [sum(counts[:i]) for i in range(len(counts))]
    return Arg(list(arrays), (sum(counts), arrays[0].shape[1]), offset=lambda here: starts, counts=counts)


def pieced(first, direct, relayed):
    base, count = first.shape[0], direct.shape[0]

    def offset(here):
        bit = here["bit"]
        return (
            0,
            pl.multiple_of(base + count * bit, 16),
            pl.multiple_of(base + count * (1 - bit), 16),
        )

    return Arg([first, direct, relayed], (base + 2 * count, first.shape[1]), offset=offset)


LIMIT = 18


def run(body, args, outs, flops, visible=None, scratch=()):
    args = [a if isinstance(a, Arg) else Arg([a], a.shape) for a in args]
    arrays = [array for a in args for array in a.arrays]
    loaded = [a for a in args if not a.held]
    stay = [isinstance(o, Held) for o in outs]
    structs = [o.struct if isinstance(o, Held) else o for o in outs]
    n_arrays, n_out, n_stored = len(arrays), len(outs), len(outs) - sum(stay)

    def kernel(*refs):
        here = {"strip": lax.axis_index("mp"), "bit": lax.axis_index("dp") & 1, "dp": lax.axis_index("dp")}
        if visible is not None:
            visible_ref, *refs = refs
            here["visible"] = visible_ref[here["strip"]]
            here["visible_across"] = visible_ref[here["strip"] ^ 2]
        ins, results, refs = refs[:n_arrays], refs[n_arrays : n_arrays + n_out], refs[n_arrays + n_out :]
        in_buffers, refs = list(refs[: len(loaded)]), refs[len(loaded) :]
        out_buffers, (in_sems, out_sems, *rest) = list(refs[:n_stored]), refs[n_stored:]
        loads, j = [], 0
        for a in args:
            if a.held:
                loads.append(Load(ins[j] if a.view is None else a.view(ins[j], here)))
                j += 1
                continue
            buffer, copies = in_buffers.pop(0), []
            offsets = a.offset(here) if a.offset is not None else None
            for i, array in enumerate(a.arrays):
                source = a.view(ins[j], here) if a.view is not None else ins[j]
                target = buffer if offsets is None else buffer.at[pl.ds(offsets[i], a.counts[i])]
                if offsets is not None and a.counts[i] < array.shape[0]:
                    source = source.at[pl.ds(0, a.counts[i])]
                copies.append(pltpu.make_async_copy(source, target, in_sems.at[j]))
                j += 1
            loads.append(Load(buffer, copies))
        stores = []
        for i, (result, stays) in enumerate(zip(results, stay)):
            stores.append(Store(result) if stays else Store(out_buffers.pop(0), result, out_sems.at[i]))
        body(here, loads, stores, *rest)
        for load in loads:
            load.ref()
        for store in stores:
            store.close()

    moved = sum(a.size * a.dtype.itemsize for a in [*arrays, *structs])
    scratches = [pltpu.VMEM(a.dims, a.arrays[0].dtype) for a in loaded]
    scratches += [pltpu.VMEM(o.shape, o.dtype) for o, stays in zip(structs, stay) if not stays]
    scratches += [pltpu.SemaphoreType.DMA((n_arrays,)), pltpu.SemaphoreType.DMA((n_out, PIECES))]
    return pl.pallas_call(
        kernel,
        in_specs=[SMEM] * (visible is not None) + [VMEM if a.held else ANY for a in args for _ in a.arrays],
        out_specs=tuple(VMEM if stays else ANY for stays in stay),
        out_shape=tuple(structs),
        scratch_shapes=scratches + list(scratch),
        cost_estimate=pl.CostEstimate(flops=flops, bytes_accessed=moved, transcendentals=0),
        compiler_params=pltpu.CompilerParams(vmem_limit_bytes=LIMIT << 20),
    )(
        *([] if visible is None else [visible]),
        *(
            array if a.held else pltpu.with_memory_space_constraint(array, pltpu.HBM)
            for a in args
            for array in a.arrays
        ),
    )


def norm_parts(values):
    center = values - jnp.mean(values, axis=-1, keepdims=True)
    rstd = lax.rsqrt(jnp.mean(center * center, axis=-1, keepdims=True) + 1e-06)
    return center * rstd, rstd


def norm_back(unit, rstd, gain, grad):
    scaled = grad * gain
    first = jnp.mean(scaled, axis=-1, keepdims=True)
    second = jnp.mean(scaled * unit, axis=-1, keepdims=True)
    return rstd * (scaled - first - unit * second)


def row_sum(values):
    return jnp.sum(values, axis=0, keepdims=True)


BIAS_EXPAND, BIAS_HEADS, GAIN_ONE, SHIFT_ONE, GAIN_TWO, SHIFT_TWO, BIAS_OUT, BIAS_REDUCE = range(8)


def vector(vectors, row):
    return vectors[row : row + 1, :].astype(F32)


def pack_body(here, ins, outs):
    pieces, b_query, b_value, *vectors = ins
    choice, first, pack, small = outs
    rows = pieces.ref()
    third = choice.shape[0]
    choice.send_from(rows.at[pl.ds(pl.multiple_of(third * (1 + here["bit"]), 16), third)])
    first.start(rows.at[pl.ds(0, third)], first.target.at[pl.ds(SMALL, third)])
    pack.send_from(rows)
    small[...] = jnp.zeros(small.shape, BF)
    part = b_query.shape[0]
    small[BIAS_HEADS : BIAS_HEADS + 1, :part] = b_query[...].reshape(1, part)
    small[BIAS_HEADS : BIAS_HEADS + 1, part : 2 * part] = b_value[...].reshape(1, part)
    rows_of_vectors = (BIAS_EXPAND, GAIN_ONE, SHIFT_ONE, GAIN_TWO, SHIFT_TWO, BIAS_OUT, BIAS_REDUCE)
    for row, values in zip(rows_of_vectors, vectors):
        small[row : row + 1, :] = values[...].reshape(1, values.shape[0])
    first.start(small.buffer, first.target.at[pl.ds(0, SMALL)])
    small.send()


def first_norm(here, ins, outs):
    tok, vectors = ins
    normed, normed_t = outs
    unit, _ = norm_parts(tok[...].astype(F32))
    low = (unit * vector(vectors, GAIN_ONE) + vector(vectors, SHIFT_ONE)).astype(BF)
    normed[...] = low
    normed_t[...] = low.T


def branch_of(here, ins, outs):
    total = outs[4]
    for i, name in enumerate(("visible", "visible_across")):
        branch, branch_t = outs[2 * i : 2 * i + 2]
        row = lax.broadcasted_iota(jnp.int32, ins[i].shape, 0)
        kept = jnp.where(row < here[name], ins[i][...].astype(F32), 0.0)
        low = kept.astype(BF)
        branch[...] = low
        branch.send()
        branch_t[...] = low.T
        branch_t.send()
        if i == 0:
            total[...] = jnp.broadcast_to(row_sum(kept), total.shape)


def heads_forward(here, normed, smalls, packs, outs):
    q_out, k_out, v_out, e_out, o_out, ctx_out = outs
    rows, width = normed.shape
    part = width // 4
    heads = part // HD
    lane = lax.broadcasted_iota(jnp.int32, (rows, HD), 1)
    row = lax.broadcasted_iota(jnp.int32, (rows, HD), 0)
    one = jnp.where(lane == 0, 1.0, 0.0).astype(BF)
    mask = jnp.where((lane == 0) & (row >= here["visible"]), -1e30, 0.0).astype(BF)
    low = normed[...]
    for s, pack in enumerate(packs):
        biases = vector(smalls[s], BIAS_HEADS)
        at = pack.shape[0] - 4 * part
        rows_q, rows_k, rows_v = (slice(at + i * part, at + (i + 1) * part) for i in range(3))
        q = (dot_nt(low, pack[rows_q, :]) + biases[:, :part]).astype(BF) * BF(HD**-0.5)
        k = dot_nt(low, pack[rows_k, :]).astype(BF)
        v = (dot_nt(low, pack[rows_v, :]) + biases[:, part : 2 * part]).astype(BF)
        for h in range(heads):
            cols = slice(h * HD, (h + 1) * HD)
            i = s * heads + h
            q_out[i, :, :HD] = q[:, cols]
            q_out[i, :, HD:] = one
            k_out[i, :, :HD] = k[:, cols]
            k_out[i, :, HD:] = mask
            v_out[i, :, :HD] = v[:, cols]
            v_out[i, :, HD:] = one
    for out in (q_out, k_out, v_out):
        out.send()
    for i in range(len(packs) * heads):
        scores = dot_nt(q_out[i], k_out[i])
        e = jnp.exp(scores - jnp.max(scores, axis=1, keepdims=True)).astype(BF)
        e_out[i] = e
        e_out.send(i)
        o = dot(e, v_out[i])
        o_out[i] = o
        ctx_out[:, i * HD : (i + 1) * HD] = (o[:, :HD] * (1.0 / o[:, HD : HD + 1])).astype(BF)
    o_out.send()
    ctx_out.send()


def heads_shapes(rows, part, slots):
    n = slots * part // HD
    outs = [Held((n, rows, 2 * HD), BF)] * 3
    return outs + [Held((n, rows, rows), BF), Held((n, rows, 2 * HD), F32), Held((rows, n * HD), BF)]


def near_attention(here, ins, outs):
    normed, small0, pack0, small1, pack1 = ins
    heads_forward(here, normed, (small0, small1), (pack0, pack1), outs)


def far_attention(here, ins, outs):
    normed, small2, pack2, small3, pack3, ctx, wo0, wo1, tok, vectors = ins
    heads_forward(here, normed, (small2, small3), (pack2, pack3), outs[:6])
    resid, normed_two, normed_two_t, *halves = outs[6:]
    part = wo0.shape[0]
    total = tok[...].astype(F32) + vector(vectors, BIAS_OUT)
    total += dot(ctx[:, :part], wo0[...]) + dot(ctx[:, part:], wo1[...])
    far = outs[5]
    total += dot(far[:, :part], pack2[-part:, :])
    total += dot(far[:, part:], pack3[-part:, :])
    resid[...] = total
    resid.send()
    unit, _ = norm_parts(total)
    low = (unit * vector(vectors, GAIN_TWO) + vector(vectors, SHIFT_TWO)).astype(BF)
    normed_two[...] = low
    count = halves[0].shape[0]
    for i, half in enumerate(halves):
        half.send_from(normed_two.buffer.at[pl.ds(i * count, count)])
    normed_two_t[...] = low.T


def hidden_of(normed, branch, small, we, wr):
    pre = dot(normed[...], we) + vector(small, BIAS_EXPAND)
    cdf = 0.5 * (1.0 + lax.erf(pre * 0.7071067811865476))
    slope = cdf + pre * (jnp.exp(-0.5 * pre * pre) * 0.3989422804014327)
    return (pre * cdf).astype(BF), (dot_nt(branch[...], wr) * slope).astype(BF)


def near_feed(here, ins, outs):
    normed, er1, branch, normed_t, branch_t, small1, er0, small0 = ins
    grad0, grad1, d_small, mlp, d_norm = outs
    units = normed.shape[1]
    total, back = None, None
    for s, (grads, er, small) in enumerate(((grad1, er1, small1), (grad0, er0, small0))):
        we, wr = er[:units, :], er[units:, :]
        hidden, d_pre = hidden_of(normed, branch, small, we, wr)
        grads[0] = dot(normed_t[...], d_pre).astype(BF)
        grads.send(0)
        grads[1] = dot(branch_t[...], hidden).astype(BF)
        grads.send(1)
        d_small[s : s + 1, :] = row_sum(d_pre.astype(F32))
        total = dot(hidden, wr) if total is None else total + dot(hidden, wr)
        back = dot_nt(d_pre, we) if back is None else back + dot_nt(d_pre, we)
    mlp[...], d_norm[...] = total, back


def cross_feed(here, ins, outs):
    normed, er1, branch, small1, er0, small0 = ins
    hidden1, d_pre1, hidden0, d_pre0, normed_t, d_norm = outs
    units = normed.shape[1]
    h, d = hidden_of(normed, branch, small1, er1[:units, :], er1[units:, :])
    hidden1[...], d_pre1[...] = h, d
    hidden1.send()
    d_pre1.send()
    back = dot_nt(d, er1[:units, :])
    h, d = hidden_of(normed, branch, small0, er0[:units, :], er0[units:, :])
    hidden0[...], d_pre0[...] = h, d
    hidden0.send()
    d_pre0.send()
    normed_t[...] = normed[...].T
    normed_t.send()
    d_norm[...] = (back + dot_nt(d, er0[:units, :])).astype(BF)


def cross_grads(here, ins, outs):
    cross_t, red1, red0, part1, part0, d_near, *halves = ins
    grad0, grad1, d_small, mlp = outs
    count = len(halves) // 2
    halves = halves[:count], halves[count:]
    rows = halves[0][0].shape[0]

    def over_halves(left, right):
        return sum(dot(left(i), right(i)) for i in range(2))

    for s, (grads, rest) in enumerate(((grad1, part1), (grad0, part0))):
        hidden, d_pre = 2 * s, 2 * s + 1
        grads[1] = (
            over_halves(lambda i: cross_t[:, i * rows : (i + 1) * rows], lambda i: halves[i][hidden][...])
            + rest[1].astype(F32)
        ).astype(BF)
        grads.send(1)
        grads[0] = (
            over_halves(lambda i: halves[i][4][...], lambda i: halves[i][d_pre][...]) + rest[0].astype(F32)
        ).astype(BF)
        grads.send(0)
        total = sum(row_sum(halves[i][d_pre][...].astype(F32)) for i in range(2))
        d_small[s : s + 1, :] = d_near[s : s + 1, :] + total
    for i in range(2):
        out = dot(halves[i][0][...], red1[...]) + dot(halves[i][2][...], red0[...])
        mlp[i * rows : (i + 1) * rows, :] = out.astype(BF)


def heads_backward(attn, attn_t, normed_t, saved, s, column, pack, grads, d_small, d_in):
    q_in, k_in, v_in, e_in, o_in, ctx = saved
    part = ctx.shape[1] // 2
    at_pack = pack.shape[0] - 4 * part
    heads = part // HD
    d_ctx = dot_nt(attn[...], pack[at_pack + 3 * part :, :]).astype(BF).astype(F32)
    back_v, back_k = [], []
    for h in range(s * heads, (s + 1) * heads):
        o = o_in[h]
        inverse = 1.0 / o[:, HD : HD + 1]
        at = h - s * heads
        do = (d_ctx[:, at * HD : (at + 1) * HD] * inverse).astype(BF)
        term = jnp.sum(do.astype(F32) * o[:, :HD], axis=1, keepdims=True) * inverse
        e = e_in[h]
        d_prob = dot_nt(do, v_in[h][:, :HD])
        d_score = (e.astype(F32) * (d_prob - term)).astype(BF)
        back_v.append(dot(do.T, e))
        back_k.append(dot(q_in[h][:, :HD].T, d_score))
        d_in[:, at * HD : (at + 1) * HD] = (dot(d_score, k_in[h][:, :HD]) * HD**-0.5).astype(BF)
    d_in[:, part : 2 * part] = jnp.concatenate(back_k, axis=0).T.astype(BF)
    d_in[:, 2 * part :] = jnp.concatenate(back_v, axis=0).T.astype(BF)
    grads[:, : 3 * part] = dot(normed_t[...], d_in[...]).astype(BF)
    grads[:, 3 * part :] = dot(attn_t[...], ctx[:, column * part : (column + 1) * part]).astype(BF)
    grads.send()
    d_small[:, :part] = row_sum(d_in[:, :part].astype(F32))
    d_small[:, part : 2 * part] = row_sum(d_in[:, 2 * part :].astype(F32))
    return dot(d_in[...], pack[at_pack : at_pack + 3 * part, :])


def small_rows(kept, sent, d_feed, d_far, d_one, d_zero, d_reduce, sums, gain, shift):
    for out in (kept, sent):
        out[...] = jnp.zeros(out.shape, F32)
        out[4:5, :] = d_reduce[0:1, :]
        out[5:8, :] = sums[0:3, :]
        out[8:9, :] = gain
        out[9:10, :] = shift
    for out, i, zero in ((sent, 0, d_one[0:1, :]), (kept, 1, d_zero)):
        out[0:1, :] = d_feed[i : i + 1, :]
        out[1:2, :] = zero
        out[3:4, :] = d_far[i : i + 1, :]


def far_back(here, ins, outs, d_in, d_row):
    resid, d_norm, got, branch, vectors, pack3, normed_t, *saved, pack2 = ins
    grad2, grad3, d_small, out, grad, attn, attn_t, sums = outs
    unit, rstd = norm_parts(resid[...])
    dn = d_norm[...] + got[...].astype(F32)
    g = branch[...].astype(F32) + norm_back(unit, rstd, vector(vectors, GAIN_TWO), dn)
    grad[...] = g
    grad.send()
    low = g.astype(BF)
    attn[...] = low
    attn.send()
    attn_t[...] = low.T
    attn_t.send()
    sums[0:1, :] = row_sum(low.astype(F32))
    sums[1:2, :] = row_sum(dn * unit)
    sums[2:3, :] = row_sum(dn)
    d_row[...] = jnp.zeros(d_row.shape, F32)
    back = heads_backward(attn, attn_t, normed_t, saved, 1, 1, pack3, grad3, d_row, d_in)
    d_small[0:1, :] = d_row[...]
    back = back + heads_backward(attn, attn_t, normed_t, saved, 0, 0, pack2, grad2, d_row, d_in)
    d_small[1:2, :] = d_row[...]
    out[...] = back


def result_body(here, ins, outs):
    resid, mlp, got, vectors = ins
    row = lax.broadcasted_iota(jnp.int32, resid.shape, 0)
    total = resid[...] + (mlp[...] + got[...].astype(F32) + vector(vectors, BIAS_REDUCE))
    outs[0][...] = jnp.where(row < here["visible"], total, 0.0).astype(BF)


def one_back(here, ins, outs, d_in, d_row):
    attn, pack, attn_t, normed_t, *saved, d_norm = ins
    grads, d_small, out = outs
    d_row[...] = jnp.zeros(d_row.shape, F32)
    dn = heads_backward(attn, attn_t, normed_t, saved, 0, 1, pack, grads, d_row, d_in)
    d_small[0:1, :] = d_row[...]
    out[...] = d_norm[...] + dn


def last_back(here, ins, outs, d_in, d_row):
    attn, pack, attn_t, normed_t, *rest = ins
    saved, (d_norm, tok, grad, vectors, *small) = rest[:6], rest[6:]
    grads, out, kept, sent = outs
    d_row[...] = jnp.zeros(d_row.shape, F32)
    dn = d_norm[...] + heads_backward(
        attn, attn_t, normed_t, saved, 0, 0, pack, grads, d_row, d_in
    )
    unit, rstd = norm_parts(tok[...].astype(F32))
    out[...] = (grad[...] + norm_back(unit, rstd, vector(vectors, GAIN_ONE), dn)).astype(BF)
    out.send()
    d_feed, d_far, d_one, d_reduce, sums = small
    gain, shift = row_sum(dn * unit), row_sum(dn)
    small_rows(kept, sent, d_feed, d_far, d_one, d_row[...], d_reduce, sums, gain, shift)


def stage_body(items, counts, here, ins, outs):
    payloads, kept = outs[: len(counts)], list(outs[len(counts) :])
    filled = [0] * len(counts)
    ins = list(ins)
    for kind, count, payload, *rest in items:
        terms, ins = ins[:count], ins[count:]
        target, start = payloads[payload], filled[payload]
        if kind == "halve":
            bit, inner = rest
            mine = (here["dp"] >> bit) & 1
            out = kept.pop(0)
            for j in range(out.shape[0] // inner):
                for side, goal, base in ((1 - mine, target, start), (mine, out, 0)):
                    rows = pl.ds(pl.multiple_of((2 * j + side) * inner, 16), inner)
                    value = sum(term[rows, :].astype(F32) for term in terms)
                    goal[base + j * inner : base + (j + 1) * inner, :] = value.astype(BF)
            filled[payload] += out.shape[0]
        elif kind == "sum":
            value = sum(term[...].astype(F32) for term in terms)
            target[start : start + value.shape[0], :] = value.astype(BF)
            filled[payload] += value.shape[0]
        else:
            value = small_sum(terms)
            kept.pop(0)[...] = value
            high = value.astype(BF)
            target[start : start + SMALL, :] = high
            target[start + SMALL : start + 2 * SMALL, :] = (value - high.astype(F32)).astype(BF)
            filled[payload] += 2 * SMALL
        if filled[payload] == counts[payload]:
            target.send()


def small_sum(terms):
    value = None
    for term in terms:
        part = term[...]
        if part.shape[0] != SMALL:
            part = part[:SMALL, :].astype(F32) + part[SMALL:, :].astype(F32)
        value = part if value is None else value + part
    return value


def item_rows(item):
    kind, terms = item[:2]
    if kind == "small":
        return 2 * SMALL
    rows = terms[0].dims[0] if isinstance(terms[0], Arg) else terms[0].shape[0]
    return rows // 2 if kind == "halve" else rows


def stage(items, width):
    n_payloads = 1 + max(item[2] for item in items)
    counts, kept, places = [0] * n_payloads, [], []
    for item in items:
        rows = item_rows(item)
        places.append((item[2], counts[item[2]], rows))
        counts[item[2]] += rows
        if item[0] == "halve":
            kept.append(Held((rows, width), BF))
        elif item[0] == "small":
            kept.append(Held((SMALL, width), F32))
    outs = [shape((count, width), BF) for count in counts] + kept
    args = [term for item in items for term in item[1]]
    specs = [(item[0], len(item[1]), *item[2:]) for item in items]
    results = run(partial(stage_body, specs, counts), args, outs, 1000)
    return results[:n_payloads], list(results[n_payloads:]), places


def final_body(part, here, ins, outs):
    expand_a, expand_b, reduce_a, reduce_b, heads_a, heads_b, heads_c, small, small_got = ins
    g_query, g_key, g_value, g_output, g_expand, g_reduce, totals = outs
    g_expand[...] = expand_a[...].astype(F32) + expand_b[...].astype(F32)
    g_expand.send()
    g_reduce[...] = (reduce_a[...].astype(F32) + reduce_b[...].astype(F32)).T
    g_reduce.send()
    value, got = small[...], small_sum([small_got])
    totals[0:2, :] = value[0:2, :] + got[2:4, :]
    totals[2:4, :] = value[2:4, :]
    totals[4:, :] = value[4:, :] + got[4:, :]
    sums = sum(v[...].astype(F32) for v in (heads_a, heads_b, heads_c))
    for i, out in enumerate((g_query, g_key, g_value)):
        out[...] = sums[:, i * part : (i + 1) * part]
        out.send()
    g_output[...] = sums[:, 3 * part :].T


def spread_body(*refs):
    ins, out, buffer, in_sems, out_sems = refs[:4], refs[4], refs[5], refs[6], refs[7]
    strip = lax.axis_index("mp")
    reads = [pltpu.make_async_copy(ins[s], buffer.at[s], in_sems.at[s]) for s in range(4)]
    writes = [pltpu.make_async_copy(buffer.at[s], out.at[strip ^ s], out_sems.at[s]) for s in range(4)]
    for read in reads:
        read.start()
    for read, write in zip(reads, writes):
        read.wait()
        write.start()
    for write in writes:
        write.wait()


def spread(strips):
    rows, width = strips[0].shape
    dtype = strips[0].dtype
    return pl.pallas_call(
        spread_body,
        in_specs=[ANY] * 4,
        out_specs=ANY,
        out_shape=shape((4, rows, width), dtype),
        scratch_shapes=[pltpu.VMEM((4, rows, width), dtype)] + [pltpu.SemaphoreType.DMA((4,))] * 2,
        cost_estimate=pl.CostEstimate(flops=0, bytes_accessed=16 * rows * width, transcendentals=0),
    )(*strips)


def swap(values, axis, size, bit):
    return lax.ppermute(values, axis, [(i, i ^ (1 << bit)) for i in range(size)])


def tie(*values):
    return lax.optimization_barrier(values)


def plain_sums(n_dp, across, part, feeds, heads, far, small):
    def scattered(values):
        total = sum(v.astype(F32) for v in values)
        return lax.psum_scatter(total, "dp", scatter_dimension=0, tiled=True)

    g_expand, g_reduce = (scattered([v[i] for v in feeds]) for i in range(2))
    total = scattered(heads) + across(scattered(far))
    g_query, g_key, g_value = (total[:, i * part : (i + 1) * part] for i in range(3))
    sums = lax.psum(small[0] + small[1], "dp")
    got = across(sums)
    totals = jnp.concatenate([sums[0:2] + got[2:4], sums[2:4], sums[4:] + got[4:]])
    return g_query, g_key, g_value, total[:, 3 * part :].T, g_expand, g_reduce.T, totals


def arranged(result, grad_tokens, part, g_query, g_key, g_value, g_output, g_expand, g_reduce, totals):
    return (
        result,
        grad_tokens,
        g_query,
        totals[1, :part],
        g_key,
        g_value,
        totals[1, part : 2 * part],
        g_output,
        totals[5],
        g_expand,
        totals[0],
        g_reduce,
        totals[4],
        totals[8],
        totals[9],
        totals[6],
        totals[7],
    )


def local(
    sizes,
    tokens,
    visible,
    w_query,
    b_query,
    w_key,
    w_value,
    b_value,
    w_output,
    b_output,
    w_expand,
    b_expand,
    w_reduce,
    b_reduce,
    gain_first,
    shift_first,
    gain_second,
    shift_second,
    cotangent,
):
    n_dp, n_mp = sizes
    part, units, (_, rows, width) = w_query.shape[1], w_expand.shape[1], tokens.shape
    core = partial(swap, axis="mp", size=n_mp, bit=0)
    across = partial(swap, axis="mp", size=n_mp, bit=1)
    over = [partial(swap, axis="dp", size=n_dp, bit=b) for b in range(n_dp.bit_length() - 1)]
    flat, tall, moved = Held((rows, width), BF), Held((width, rows), BF), shape((rows, width), BF)
    wide, rows8, rows16 = Held((rows, width), F32), Held((8, width), F32), shape((SMALL, width), F32)
    flop = 2 * rows * width * width
    block = width // n_dp
    halving = n_dp == 8 and block % 16 == 0

    third = 4 * part // 3
    direct, first, pack0, small0 = run(
        pack_body,
        (
            stacked(w_query.T, w_key.T, w_value.T, w_output),
            b_query,
            b_value,
            b_expand,
            gain_first,
            shift_first,
            gain_second,
            shift_second,
            b_output,
            b_reduce,
        ),
        [
            shape((third, width), BF),
            shape((SMALL + third, width), BF),
            shape((4 * part, width), BF),
            shape((SMALL, width), BF),
        ],
        1000,
    )
    direct, first, pack1, small1 = across(direct), across(first), core(pack0), core(small0)
    n1, n1t = run(first_norm, (own(tokens), small0), (flat, tall), flop // 100)
    n1, pack1, small1 = tie(n1, pack1, small1)
    near = run(near_attention, (held(n1), small0, pack0, small1, pack1), heads_shapes(rows, part, 2), 2 * flop, visible)
    *near, n1, direct, w_exp, w_red, cot = tie(*near, n1, direct, w_expand, w_reduce, cotangent)
    relayed, direct3 = over[0](direct), core(direct)
    exp1, red1 = core(w_exp), core(w_red)
    branch, branch_t, cross, cross_t, d_reduce = run(
        branch_of, (own(cot), other(cot)), (flat, tall, flat, tall, rows8), flop // 100, visible
    )
    branch, first, relayed = tie(branch, first, relayed)
    pack2, pack3 = (first, direct, relayed), (core(first), direct3, core(relayed))
    *pack3, branch, n1 = tie(*pack3, branch, n1)
    small2, small3 = rows_of(pack2[0], 0, SMALL), rows_of(pack3[0], 0, SMALL)
    pack2, pack3 = pieced(*pack2), pieced(*pack3)
    half, half_t = Held((rows // 2, width), BF), Held((width, rows // 2), BF)
    half_moved = shape((rows // 2, width), BF)
    *away, resid, n2, n2t, n2a, n2b = run(
        far_attention,
        (
            held(n1),
            small2,
            pack2,
            small3,
            pack3,
            held(near[5]),
            rows_of(pack0, 3 * part, part),
            rows_of(pack1, 3 * part, part),
            own(tokens),
            small0,
        ),
        [*heads_shapes(rows, part, 2), wide, flat, tall, half_moved, half_moved],
        3 * flop,
        visible,
    )
    n2, exp1, red1 = tie(n2, exp1, red1)
    n2a, n2b = across(n2a), across(n2b)
    grads = shape((2, width, units), BF)
    own_er, core_er = stacked(w_exp, w_red), stacked(exp1, red1)
    g0, g1, de_near, mlp, dn2 = run(
        near_feed,
        (held(n2), core_er, held(branch), held(n2t), held(branch_t), small1, own_er, small0),
        [grads, grads, rows8, wide, wide],
        12 * flop,
    )

    def cross_half(normed, first):
        return run(
            cross_feed,
            (normed, core_er, held(cross, first, rows // 2), small1, own_er, small0),
            [half, half, half, half, half_t, half_moved],
            3 * flop,
        )

    g0, g1, n2a = tie(g0, g1, n2a)
    *half_a, dn2_back = cross_half(n2a, 0)
    got_a = across(dn2_back)
    half_a[0], n2b = tie(half_a[0], n2b)
    *half_b, dn2_back = cross_half(n2b, rows // 2)
    got_b = across(dn2_back)
    half_b[0], got_a = tie(half_b[0], got_a)
    g0, g1, de_all, mlp_back = run(
        cross_grads,
        (held(cross_t), red1, w_red, g1, g0, held(de_near), *map(held, [*half_a, *half_b])),
        [grads, grads, rows8, moved],
        6 * flop,
    )
    g0, g1, mlp_back, got_b = tie(g0, g1, mlp_back, got_b)
    got0, mlp_got = core(g1), across(mlp_back)
    grads = shape((width, 4 * part), BF)
    extra = (pltpu.VMEM((rows, 3 * part), BF), pltpu.VMEM((1, width), F32))
    h2, h3, ds_far, dn1, grad_resid, attn, attn_t, sums2 = run(
        far_back,
        (held(resid), held(dn2), stacked(got_a, got_b), held(branch), small0, pack3, held(n1t), *map(held, away), pack2),
        [grads, grads, rows8, wide, wide, flat, tall, rows8],
        8 * flop,
        scratch=extra,
    )
    got_h2 = core(h3)
    h2, attn, got0 = tie(h2, attn, got0)
    if halving:
        (pay_x, pay_z), (kept_e, kept_r), _ = stage(
            [
                ("halve", (entry(g0, 0), entry(got0, 0)), 0, 0, block),
                ("halve", (entry(g0, 1), entry(got0, 1)), 1, 1, 2 * block),
            ],
            width,
        )
        got_e, got_r = over[0](pay_x), over[1](pay_z)
        kept_e, mlp_got = tie(kept_e, mlp_got)
    (strip,) = run(result_body, (held(resid), held(mlp), mlp_got, small0), [moved], flop // 100, visible)
    strip_near, strip_far = core(strip), across(strip)
    attn, strip = tie(attn, strip)

    def near_saved(s):
        n = part // HD
        return [held(a, s * n, n) for a in near[:5]] + [held(near[5])]

    def piece_of(array, place):
        return rows_of(array, place[1], place[2])

    h1, ds1, dn1 = run(
        one_back,
        (held(attn), pack1, held(attn_t), held(n1t), *near_saved(1), held(dn1)),
        [grads, rows8, wide],
        4 * flop,
        scratch=extra,
    )
    got_h0 = core(h1)
    if halving:
        attn, got_e, got_r, kept_e, got_h2 = tie(attn, got_e, got_r, kept_e, got_h2)
        (pay_z, pay_x), (kept_e, kept_r, kept_h), places_x = stage(
            [
                ("halve", (held(kept_e), got_e), 0, 1, block),
                ("halve", (held(kept_r), got_r), 1, 0, block),
                ("halve", (h2, got_h2), 1, 0, block),
            ],
            width,
        )
        got_z, got_x = over[1](pay_z), over[0](pay_x)
        attn, kept_e = tie(attn, kept_e)
    attn, strip_near, strip_far = tie(attn, strip_near, strip_far)
    strip_diag = core(strip_far)
    h0, grad_strip, small_kept, small_sent = run(
        last_back,
        (
            held(attn),
            pack0,
            held(attn_t),
            held(n1t),
            *near_saved(0),
            held(dn1),
            own(tokens),
            held(grad_resid),
            small0,
            *map(held, (de_all, ds_far, ds1, d_reduce, sums2)),
        ),
        [grads, moved, rows16, rows16],
        4 * flop,
        scratch=extra,
    )
    small_got, grad_far, grad_near = core(small_sent), across(grad_strip), core(grad_strip)
    if not halving:
        result = spread([strip, strip_near, strip_far, strip_diag])
        grad_tokens = spread([grad_strip, grad_near, grad_far, core(grad_far)])
        sums = plain_sums(n_dp, across, part, (g0, got0), (h0, got_h0), (h2, got_h2), (small_kept, small_got))
        return arranged(result, grad_tokens, part, *sums)
    h0, small_got, got_h0, got_z, got_x, strip_diag = tie(h0, small_got, got_h0, got_z, got_x, strip_diag)
    (pay_x, pay_z, pay_w), (kept_h0, small_total, kept_h, kept_e, kept_r), places = stage(
        [
            ("halve", (h0, got_h0), 0, 0, block),
            ("small", (small_kept, small_got), 0),
            ("halve", (held(kept_h), piece_of(got_x, places_x[2])), 1, 1, block),
            ("halve", (held(kept_e), got_z), 2, 2, block),
            ("halve", (held(kept_r), piece_of(got_x, places_x[1])), 2, 2, block),
        ],
        width,
    )
    got_x, got_z, got_w = over[0](pay_x), over[1](pay_z), over[2](pay_w)
    places_x, places_w = places[:2], places[3:]
    kept_h0, strip = tie(kept_h0, strip)
    result = spread([strip, strip_near, strip_far, strip_diag])
    kept_h0, got_x, got_z, got_w, result = tie(kept_h0, got_x, got_z, got_w, result)
    (pay_z, pay_h), (kept_h0, small_total, kept_h), places_z = stage(
        [
            ("halve", (held(kept_h0), piece_of(got_x, places_x[0])), 0, 1, block),
            ("small", (held(small_total), piece_of(got_x, places_x[1])), 0),
            ("halve", (held(kept_h), got_z), 1, 2, block),
        ],
        width,
    )
    got_z, got_h = over[1](pay_z), over[2](pay_h)
    kept_h0, got_z, grad_far, got_h = tie(kept_h0, got_z, grad_far, got_h)
    grad_diag = core(grad_far)
    (pay_w,), (kept_h0, small_total), places_s = stage(
        [
            ("halve", (held(kept_h0), piece_of(got_z, places_z[0])), 0, 2, block),
            ("small", (held(small_total), piece_of(got_z, places_z[1])), 0),
        ],
        width,
    )
    got_s = over[2](pay_w)
    kept_h0, grad_diag = tie(kept_h0, grad_diag)
    grad_tokens = spread([grad_strip, grad_near, grad_far, grad_diag])
    kept_h0, got_s, grad_tokens = tie(kept_h0, got_s, grad_tokens)
    (pay_y,), (small_total,), places_y = stage(
        [
            ("sum", (held(kept_h), got_h), 0),
            ("small", (held(small_total), piece_of(got_s, places_s[1])), 0),
        ],
        width,
    )
    got_y = across(pay_y)
    narrow, thin = shape((block, part), F32), shape((part, block), F32)
    sums = run(
        partial(final_body, part),
        (
            held(kept_e),
            piece_of(got_w, places_w[0]),
            held(kept_r),
            piece_of(got_w, places_w[1]),
            held(kept_h0),
            piece_of(got_s, places_s[0]),
            piece_of(got_y, places_y[0]),
            held(small_total),
            piece_of(got_y, places_y[1]),
        ),
        [narrow, narrow, narrow, thin, shape((block, units), F32), shape((units, block), F32), rows16],
        1000,
    )
    return arranged(result, grad_tokens, part, *sums)


def solution(mesh):
    placed = (
        P("dp", None, None),
        P("dp"),
        P(None, "mp"),
        P("mp"),
        P(None, "mp"),
        P(None, "mp"),
        P("mp"),
        P("mp", None),
        P(),
        P(None, "mp"),
        P("mp"),
        P("mp", None),
        P(),
        P(),
        P(),
        P(),
        P(),
        P("dp", None, None),
    )
    return jax.shard_map(
        partial(local, (mesh.shape["dp"], mesh.shape["mp"])),
        mesh=mesh,
        in_specs=placed,
        out_specs=(
            P("dp", None, None),
            P("dp", None, None),
            P("dp", "mp"),
            P("mp"),
            P("dp", "mp"),
            P("dp", "mp"),
            P("mp"),
            P("mp", "dp"),
            P(),
            P("dp", "mp"),
            P("mp"),
            P("mp", "dp"),
            P(),
            P(),
            P(),
            P(),
            P(),
        ),
        check_vma=False,
    )
```

```python
from functools import partial

import jax
import jax.numpy as jnp
from jax import lax
from jax.experimental import pallas as pl
from jax.experimental.pallas import tpu as pltpu
from jax.sharding import PartitionSpec as P

HD = 64
F32 = jnp.float32
BF = jnp.bfloat16
NT = (((1,), (1,)), ((), ()))
ANY = pl.BlockSpec(memory_space=pl.ANY)
SMEM = pl.BlockSpec(memory_space=pltpu.SMEM)
VMEM = pl.BlockSpec(memory_space=pltpu.VMEM)


def dot(left, right):
    return jnp.dot(left, right, preferred_element_type=F32)


def dot_nt(left, right):
    return lax.dot_general(left, right, NT, preferred_element_type=F32)


def shape(dims, dtype):
    return jax.ShapeDtypeStruct(dims, dtype)


class Load:
    def __init__(self, buffer, copies=()):
        self.buffer, self.copies = buffer, copies
        for copy in copies:
            copy.start()

    def ref(self):
        for copy in self.copies:
            copy.wait()
        self.copies = ()
        return self.buffer

    def __getitem__(self, index):
        return self.ref()[index]

    @property
    def shape(self):
        return self.buffer.shape


class Store:
    def __init__(self, buffer, target=None, sems=None):
        self.target, self.buffer, self.sems = target, buffer, sems
        self.copies = []

    def start(self, source, target):
        self.copies.append(pltpu.make_async_copy(source, target, self.sems.at[len(self.copies)]))
        self.copies[-1].start()

    def send(self, *index):
        if self.target is not None:
            self.start(*((self.buffer.at[index], self.target.at[index]) if index else (self.buffer, self.target)))

    def send_from(self, view):
        self.start(view, self.target)

    def close(self):
        if not self.copies:
            self.send()
        for copy in self.copies:
            copy.wait()

    def __setitem__(self, index, value):
        self.buffer[index] = value

    def __getitem__(self, index):
        return self.buffer[index]

    @property
    def shape(self):
        return self.buffer.shape


class Held:
    def __init__(self, dims, dtype):
        self.struct = shape(dims, dtype)


PIECES = 8
SMALL = 16


class Arg:
    def __init__(self, arrays, dims, view=None, offset=None, counts=None, held=False, firsts=None, fixed=False):
        self.arrays, self.dims, self.view, self.offset, self.held = arrays, dims, view, offset, held
        self.fixed = fixed
        self.firsts = firsts or [0] * len(arrays)
        self.counts = counts or [a.shape[0] for a in arrays]


def own(array):
    return Arg([array], array.shape[1:], view=lambda ref, here: ref.at[here["strip"]], fixed=True)


def other(array):
    return Arg([array], array.shape[1:], view=lambda ref, here: ref.at[here["strip"] ^ 2], fixed=True)


def entry(array, index):
    return Arg([array], array.shape[1:], view=lambda ref, here: ref.at[index])


def held(array, first=None, count=None):
    if first is None:
        return Arg([array], array.shape, held=True)
    view = lambda ref, here: ref.at[pl.ds(first, count)]
    return Arg([array], (count, *array.shape[1:]), view=view, held=True)


def rows_of(array, first, count):
    return Arg([array], (count, *array.shape[1:]), view=lambda ref, here: ref.at[pl.ds(first, count)])


def stacked(*arrays, counts=None, fixed=False):
    counts = counts or [a.shape[0] for a in arrays]
    starts = [sum(counts[:i]) for i in range(len(counts))]
    dims = (sum(counts), arrays[0].shape[1])
    return Arg(list(arrays), dims, offset=lambda here: starts, counts=counts, fixed=fixed)


def pieced(first, direct, relayed):
    base, count = first.shape[0], direct.shape[0]

    def offset(here):
        bit = here["bit"]
        return (
            0,
            pl.multiple_of(base + count * bit, 16),
            pl.multiple_of(base + count * (1 - bit), 16),
        )

    return Arg([first, direct, relayed], (base + 2 * count, first.shape[1]), offset=offset)


LIMIT = 18


def run(body, args, outs, flops, visible=None, scratch=()):
    args = [a if isinstance(a, Arg) else Arg([a], a.shape) for a in args]
    arrays = [array for a in args for array in a.arrays]
    loaded = [a for a in args if not a.held]
    stay = [isinstance(o, Held) for o in outs]
    structs = [o.struct if isinstance(o, Held) else o for o in outs]
    n_arrays, n_out, n_stored = len(arrays), len(outs), len(outs) - sum(stay)

    def kernel(*refs):
        here = {"strip": lax.axis_index("mp"), "bit": lax.axis_index("dp") & 1, "dp": lax.axis_index("dp")}
        if visible is not None:
            visible_ref, *refs = refs
            here["visible"] = visible_ref[here["strip"]]
            here["visible_across"] = visible_ref[here["strip"] ^ 2]
        ins, results, refs = refs[:n_arrays], refs[n_arrays : n_arrays + n_out], refs[n_arrays + n_out :]
        in_buffers, refs = list(refs[: len(loaded)]), refs[len(loaded) :]
        out_buffers, (in_sems, out_sems, *rest) = list(refs[:n_stored]), refs[n_stored:]
        loads, j = [], 0
        for a in args:
            if a.held:
                loads.append(Load(ins[j] if a.view is None else a.view(ins[j], here)))
                j += 1
                continue
            buffer, copies = in_buffers.pop(0), []
            offsets = a.offset(here) if a.offset is not None else None
            for i, array in enumerate(a.arrays):
                source = a.view(ins[j], here) if a.view is not None else ins[j]
                target = buffer if offsets is None else buffer.at[pl.ds(offsets[i], a.counts[i])]
                if offsets is not None and a.counts[i] < array.shape[0]:
                    source = source.at[pl.ds(a.firsts[i], a.counts[i])]
                copies.append(pltpu.make_async_copy(source, target, in_sems.at[j]))
                j += 1
            loads.append(Load(buffer, copies))
        stores = []
        for i, (result, stays) in enumerate(zip(results, stay)):
            stores.append(Store(result) if stays else Store(out_buffers.pop(0), result, out_sems.at[i]))
        body(here, loads, stores, *rest)
        for load in loads:
            load.ref()
        for store in stores:
            store.close()

    moved = sum(a.size * a.dtype.itemsize for a in [*arrays, *structs])
    scratches = [pltpu.VMEM(a.dims, a.arrays[0].dtype) for a in loaded]
    scratches += [pltpu.VMEM(o.shape, o.dtype) for o, stays in zip(structs, stay) if not stays]
    scratches += [pltpu.SemaphoreType.DMA((n_arrays,)), pltpu.SemaphoreType.DMA((n_out, PIECES))]
    return pl.pallas_call(
        kernel,
        in_specs=[SMEM] * (visible is not None) + [VMEM if a.held else ANY for a in args for _ in a.arrays],
        out_specs=tuple(VMEM if stays else ANY for stays in stay),
        out_shape=tuple(structs),
        scratch_shapes=scratches + list(scratch),
        cost_estimate=pl.CostEstimate(flops=flops, bytes_accessed=moved, transcendentals=0),
        compiler_params=pltpu.CompilerParams(vmem_limit_bytes=LIMIT << 20),
    )(
        *([] if visible is None else [visible]),
        *(
            pltpu.with_memory_space_constraint(array, pltpu.HBM) if a.fixed else array
            for a in args
            for array in a.arrays
        ),
    )


def norm_parts(values):
    center = values - jnp.mean(values, axis=-1, keepdims=True)
    rstd = lax.rsqrt(jnp.mean(center * center, axis=-1, keepdims=True) + 1e-06)
    return center * rstd, rstd


def norm_back(unit, rstd, gain, grad):
    scaled = grad * gain
    first = jnp.mean(scaled, axis=-1, keepdims=True)
    second = jnp.mean(scaled * unit, axis=-1, keepdims=True)
    return rstd * (scaled - first - unit * second)


def row_sum(values):
    return jnp.sum(values, axis=0, keepdims=True)


BIAS_EXPAND, BIAS_HEADS, GAIN_ONE, SHIFT_ONE, GAIN_TWO, SHIFT_TWO, BIAS_OUT, BIAS_REDUCE = range(8)


def vector(vectors, row):
    return vectors[row : row + 1, :].astype(F32)


def pack_body(here, ins, outs):
    pieces, b_query, b_value, *vectors = ins
    choice, first, pack, small = outs
    rows = pieces.ref()
    third = choice.shape[0]
    choice.send_from(rows.at[pl.ds(pl.multiple_of(third * (1 + here["bit"]), 16), third)])
    first.start(rows.at[pl.ds(0, third)], first.target.at[pl.ds(SMALL, third)])
    pack.send_from(rows)
    small[...] = jnp.zeros(small.shape, BF)
    part = b_query.shape[0]
    small[BIAS_HEADS : BIAS_HEADS + 1, :part] = b_query[...].reshape(1, part)
    small[BIAS_HEADS : BIAS_HEADS + 1, part : 2 * part] = b_value[...].reshape(1, part)
    rows_of_vectors = (BIAS_EXPAND, GAIN_ONE, SHIFT_ONE, GAIN_TWO, SHIFT_TWO, BIAS_OUT, BIAS_REDUCE)
    for row, values in zip(rows_of_vectors, vectors):
        small[row : row + 1, :] = values[...].reshape(1, values.shape[0])
    first.start(small.buffer, first.target.at[pl.ds(0, SMALL)])
    small.send()


def first_norm(here, ins, outs):
    tok, vectors = ins
    normed, normed_t = outs
    unit, _ = norm_parts(tok[...].astype(F32))
    low = (unit * vector(vectors, GAIN_ONE) + vector(vectors, SHIFT_ONE)).astype(BF)
    normed[...] = low
    normed_t[...] = low.T


def branch_of(here, ins, outs):
    cot, cross, red0, red1 = ins
    total, hidden = outs[4], outs[5:]
    for i, (strip, name) in enumerate(((cot, "visible"), (cross, "visible_across"))):
        branch, branch_t = outs[2 * i : 2 * i + 2]
        row = lax.broadcasted_iota(jnp.int32, strip.shape, 0)
        kept = jnp.where(row < here[name], strip[...].astype(F32), 0.0)
        low = kept.astype(BF)
        branch[...] = low
        branch_t[...] = low.T
        hidden[2 * i][...] = dot_nt(low, red0[...]).astype(BF)
        hidden[2 * i + 1][...] = dot_nt(low, red1[...]).astype(BF)
        if i == 0:
            total[...] = jnp.broadcast_to(row_sum(kept), total.shape)


def heads_forward(here, normed, smalls, packs, outs):
    q_out, k_out, v_out, e_out, o_out, ctx_out = outs
    rows, width = normed.shape
    part = width // 4
    heads = part // HD
    lane = lax.broadcasted_iota(jnp.int32, (rows, HD), 1)
    row = lax.broadcasted_iota(jnp.int32, (rows, HD), 0)
    one = jnp.where(lane == 0, 1.0, 0.0).astype(BF)
    mask = jnp.where((lane == 0) & (row >= here["visible"]), -1e30, 0.0).astype(BF)
    low = normed[...]
    for s, pack in enumerate(packs):
        biases = vector(smalls[s], BIAS_HEADS)
        at = pack.shape[0] - 4 * part
        rows_q, rows_k, rows_v = (slice(at + i * part, at + (i + 1) * part) for i in range(3))
        q = (dot_nt(low, pack[rows_q, :]) + biases[:, :part]).astype(BF) * BF(HD**-0.5)
        k = dot_nt(low, pack[rows_k, :]).astype(BF)
        v = (dot_nt(low, pack[rows_v, :]) + biases[:, part : 2 * part]).astype(BF)
        for h in range(heads):
            cols = slice(h * HD, (h + 1) * HD)
            i = s * heads + h
            q_out[i, :, :HD] = q[:, cols]
            q_out[i, :, HD:] = one
            k_out[i, :, :HD] = k[:, cols]
            k_out[i, :, HD:] = mask
            v_out[i, :, :HD] = v[:, cols]
            v_out[i, :, HD:] = one
    for out in (q_out, k_out, v_out):
        out.send()
    for i in range(len(packs) * heads):
        scores = dot_nt(q_out[i], k_out[i])
        e = jnp.exp(scores - jnp.max(scores, axis=1, keepdims=True)).astype(BF)
        e_out[i] = e
        e_out.send(i)
        o = dot(e, v_out[i])
        o_out[i] = o
        ctx_out[:, i * HD : (i + 1) * HD] = (o[:, :HD] * (1.0 / o[:, HD : HD + 1])).astype(BF)
    o_out.send()
    ctx_out.send()


def heads_shapes(rows, part, slots):
    n = slots * part // HD
    outs = [Held((n, rows, 2 * HD), BF)] * 3
    return outs + [Held((n, rows, rows), BF), Held((n, rows, 2 * HD), F32), Held((rows, n * HD), BF)]


def near_attention(here, ins, outs):
    normed, small0, pack0, small1, pack1 = ins
    heads_forward(here, normed, (small0, small1), (pack0, pack1), outs)


def far_attention(here, ins, outs):
    normed, small2, pack2, small3, pack3, ctx, wo0, wo1, tok, vectors = ins
    heads_forward(here, normed, (small2, small3), (pack2, pack3), outs[:6])
    resid, normed_two, normed_two_t, *halves = outs[6:]
    part = wo0.shape[0]
    total = tok[...].astype(F32) + vector(vectors, BIAS_OUT)
    total += dot(ctx[:, :part], wo0[...]) + dot(ctx[:, part:], wo1[...])
    far = outs[5]
    total += dot(far[:, :part], pack2[-part:, :])
    total += dot(far[:, part:], pack3[-part:, :])
    resid[...] = total
    resid.send()
    unit, _ = norm_parts(total)
    low = (unit * vector(vectors, GAIN_TWO) + vector(vectors, SHIFT_TWO)).astype(BF)
    normed_two[...] = low
    count = halves[0].shape[0]
    for i, half in enumerate(halves):
        half.send_from(normed_two.buffer.at[pl.ds(i * count, count)])
    normed_two_t[...] = low.T


def hidden_of(normed, d_hidden, small, we):
    pre = dot(normed[...], we[...]) + vector(small, BIAS_EXPAND)
    cdf = 0.5 * (1.0 + lax.erf(pre * 0.7071067811865476))
    slope = cdf + pre * (jnp.exp(-0.5 * pre * pre) * 0.3989422804014327)
    return (pre * cdf).astype(BF), (d_hidden[...].astype(F32) * slope).astype(BF)


def near_feed(here, ins, outs):
    normed, exp1, exp0, red1, red0, d_hidden1, d_hidden0, normed_t, branch_t, small1, small0 = ins
    grad0, grad1, d_small, mlp, d_norm = outs
    total, back = None, None
    for s, (grads, we, wr, d_hidden, small) in enumerate(
        ((grad1, exp1, red1, d_hidden1, small1), (grad0, exp0, red0, d_hidden0, small0))
    ):
        hidden, d_pre = hidden_of(normed, d_hidden, small, we)
        grads[0] = dot(normed_t[...], d_pre).astype(BF)
        grads.send(0)
        grads[1] = dot(branch_t[...], hidden).astype(BF)
        grads.send(1)
        d_small[s : s + 1, :] = row_sum(d_pre.astype(F32))
        out = dot(hidden, wr[...])
        total = out if total is None else total + out
        out = dot_nt(d_pre, we[...])
        back = out if back is None else back + out
    mlp[...], d_norm[...] = total, back


def cross_feed(here, ins, outs):
    normed, exp1, exp0, d_hidden1, d_hidden0, small1, small0 = ins
    hidden1, d_pre1, hidden0, d_pre0, normed_t, d_norm = outs
    h, d = hidden_of(normed, d_hidden1, small1, exp1)
    hidden1[...], d_pre1[...] = h, d
    back = dot_nt(d, exp1[...])
    h, d = hidden_of(normed, d_hidden0, small0, exp0)
    hidden0[...], d_pre0[...] = h, d
    normed_t[...] = normed[...].T
    d_norm[...] = (back + dot_nt(d, exp0[...])).astype(BF)


def cross_slot(grads, d_small, cross_t, part, d_near, halves, hidden, d_pre):
    rows = halves[0][0].shape[0]

    def over_halves(left, right):
        return sum(dot(left(i), right(i)) for i in range(2))

    grads[1] = (
        over_halves(lambda i: cross_t[:, i * rows : (i + 1) * rows], lambda i: halves[i][hidden][...])
        + part[1].astype(F32)
    ).astype(BF)
    grads.send(1)
    grads[0] = (
        over_halves(lambda i: halves[i][-1][...], lambda i: halves[i][d_pre][...]) + part[0].astype(F32)
    ).astype(BF)
    grads.send(0)
    d_small[0:1, :] = d_near + sum(row_sum(halves[i][d_pre][...].astype(F32)) for i in range(2))


def cross_one(here, ins, outs):
    cross_t, part, d_near, *halves = ins
    count = len(halves) // 2
    cross_slot(outs[0], outs[1], cross_t, part, d_near[0:1, :], (halves[:count], halves[count:]), 0, 1)


def cross_zero(here, ins, outs):
    cross_t, part, d_near, red1, red0, *halves = ins
    grads, d_small, mlp = outs
    count = len(halves) // 2
    halves = halves[:count], halves[count:]
    rows = halves[0][0].shape[0]
    cross_slot(grads, d_small, cross_t, part, d_near[1:2, :], halves, 1, 2)
    for i in range(2):
        out = dot(halves[i][0][...], red1[...]) + dot(halves[i][1][...], red0[...])
        mlp[i * rows : (i + 1) * rows, :] = out.astype(BF)


def heads_backward(attn, attn_t, normed_t, saved, s, column, pack, grads, d_small, d_in):
    q_in, k_in, v_in, e_in, o_in, ctx = saved
    part = ctx.shape[1] // 2
    at_pack = pack.shape[0] - 4 * part
    heads = part // HD
    d_ctx = dot_nt(attn[...], pack[at_pack + 3 * part :, :]).astype(BF).astype(F32)
    back_v, back_k = [], []
    for h in range(s * heads, (s + 1) * heads):
        o = o_in[h]
        inverse = 1.0 / o[:, HD : HD + 1]
        at = h - s * heads
        do = (d_ctx[:, at * HD : (at + 1) * HD] * inverse).astype(BF)
        term = jnp.sum(do.astype(F32) * o[:, :HD], axis=1, keepdims=True) * inverse
        e = e_in[h]
        d_prob = dot_nt(do, v_in[h][:, :HD])
        d_score = (e.astype(F32) * (d_prob - term)).astype(BF)
        back_v.append(dot(do.T, e))
        back_k.append(dot(q_in[h][:, :HD].T, d_score))
        d_in[:, at * HD : (at + 1) * HD] = (dot(d_score, k_in[h][:, :HD]) * HD**-0.5).astype(BF)
    d_in[:, part : 2 * part] = jnp.concatenate(back_k, axis=0).T.astype(BF)
    d_in[:, 2 * part :] = jnp.concatenate(back_v, axis=0).T.astype(BF)
    grads[:, : 3 * part] = dot(normed_t[...], d_in[...]).astype(BF)
    grads[:, 3 * part :] = dot(attn_t[...], ctx[:, column * part : (column + 1) * part]).astype(BF)
    grads.send()
    d_small[:, :part] = row_sum(d_in[:, :part].astype(F32))
    d_small[:, part : 2 * part] = row_sum(d_in[:, 2 * part :].astype(F32))
    return dot(d_in[...], pack[at_pack : at_pack + 3 * part, :])


def far_back(here, ins, outs, d_in, d_row):
    resid, d_norm, got, branch, vectors, pack3, normed_t, *saved, pack2 = ins
    grad2, grad3, d_small, out, grad, attn, attn_t, sums = outs
    unit, rstd = norm_parts(resid[...])
    dn = d_norm[...] + got[...].astype(F32)
    g = branch[...].astype(F32) + norm_back(unit, rstd, vector(vectors, GAIN_TWO), dn)
    grad[...] = g
    grad.send()
    low = g.astype(BF)
    attn[...] = low
    attn.send()
    attn_t[...] = low.T
    attn_t.send()
    sums[0:1, :] = row_sum(low.astype(F32))
    sums[1:2, :] = row_sum(dn * unit)
    sums[2:3, :] = row_sum(dn)
    d_row[...] = jnp.zeros(d_row.shape, F32)
    back = heads_backward(attn, attn_t, normed_t, saved, 1, 1, pack3, grad3, d_row, d_in)
    d_small[0:1, :] = d_row[...]
    back = back + heads_backward(attn, attn_t, normed_t, saved, 0, 0, pack2, grad2, d_row, d_in)
    d_small[1:2, :] = d_row[...]
    out[...] = back


def result_body(here, ins, outs):
    resid, mlp, got, vectors = ins
    row = lax.broadcasted_iota(jnp.int32, resid.shape, 0)
    total = resid[...] + (mlp[...] + got[...].astype(F32) + vector(vectors, BIAS_REDUCE))
    outs[0][...] = jnp.where(row < here["visible"], total, 0.0).astype(BF)


class Rows:
    def __init__(self, parts):
        self.parts = parts

    def __setitem__(self, index, value):
        rows, columns = index
        start = 0
        for part in self.parts:
            count = part.shape[0]
            part[:, columns] = value[start : start + count, :]
            start += count

    def send(self):
        for part in self.parts:
            part.send()


def slot_back(column, here, ins, outs, d_in, d_row):
    attn, pack, attn_t, normed_t, *saved, d_norm = ins
    grads, (d_small, out) = Rows(outs[:-2]), outs[-2:]
    d_row[...] = jnp.zeros(d_row.shape, F32)
    dn = heads_backward(attn, attn_t, normed_t, saved, 0, column, pack, grads, d_row, d_in)
    d_small[0:1, :] = d_row[...]
    out[...] = d_norm[...] + dn


def last_back(here, ins, outs, d_in, d_row):
    attn, pack, attn_t, normed_t, *rest = ins
    saved, (d_norm, tok, grad, vectors, *small) = rest[:6], rest[6:]
    grads, out, small_out = outs
    d_row[...] = jnp.zeros(d_row.shape, F32)
    dn = d_norm[...] + heads_backward(
        attn, attn_t, normed_t, saved, 0, 0, pack, grads, d_row, d_in
    )
    unit, rstd = norm_parts(tok[...].astype(F32))
    out[...] = (grad[...] + norm_back(unit, rstd, vector(vectors, GAIN_ONE), dn)).astype(BF)
    out.send()
    feed0, feed1, d_far, d_one, d_reduce, sums = small
    small_out[...] = jnp.zeros(small_out.shape, F32)
    late = [feed0[0:1, :], d_row[...], feed1[0:1, :], d_one[0:1, :], d_far[1:2, :], d_far[0:1, :]]
    late += [d_reduce[0:1, :], sums[0:3, :], row_sum(dn * unit), row_sum(dn)]
    start = 0
    for values in late:
        small_out[start : start + values.shape[0], :] = values
        start += values.shape[0]


def stage_body(items, counts, here, ins, outs):
    payloads, kept = outs[: len(counts)], list(outs[len(counts) :])
    filled = [0] * len(counts)
    ins = list(ins)
    for kind, count, payload, *rest in items:
        terms, ins = ins[:count], ins[count:]
        target, start = payloads[payload], filled[payload]
        if kind == "halve":
            bit, inner = rest
            mine = (here["dp"] >> bit) & 1
            out = kept.pop(0)
            for j in range(out.shape[0] // inner):
                for side, goal, base in ((1 - mine, target, start), (mine, out, 0)):
                    rows = pl.ds(pl.multiple_of((2 * j + side) * inner, 16), inner)
                    value = sum(term[rows, :].astype(F32) for term in terms)
                    goal[base + j * inner : base + (j + 1) * inner, :] = value.astype(BF)
            filled[payload] += out.shape[0]
        else:
            value = sum(term[...].astype(F32) for term in terms)
            target[start : start + value.shape[0], :] = value.astype(BF)
            filled[payload] += value.shape[0]
        if filled[payload] == counts[payload]:
            target.send()


def item_rows(item):
    kind, terms = item[:2]
    rows = terms[0].dims[0] if isinstance(terms[0], Arg) else terms[0].shape[0]
    return rows // 2 if kind == "halve" else rows


def stage(items, width):
    n_payloads = 1 + max(item[2] for item in items)
    counts, kept, places = [0] * n_payloads, [], []
    for item in items:
        rows = item_rows(item)
        places.append((item[2], counts[item[2]], rows))
        counts[item[2]] += rows
        if item[0] == "halve":
            kept.append(Held((rows, width), BF))
    outs = [shape((count, width), BF) for count in counts] + kept
    args = [term for item in items for term in item[1]]
    specs = [(item[0], len(item[1]), *item[2:]) for item in items]
    results = run(partial(stage_body, specs, counts), args, outs, 1000)
    return results[:n_payloads], list(results[n_payloads:]), places


def small_total(own, near, far, diagonal):
    shared = own[6:, :] + near[6:, :] + far[6:, :] + diagonal[6:, :]
    return own[0:1, :] + near[2:3, :], own[1:2, :] + near[3:4, :] + far[4:5, :] + diagonal[5:6, :], shared


def small_body(here, ins, outs):
    expand, heads, shared = small_total(*ins)
    outs[0][0:1, :] = expand
    outs[0][1:2, :] = heads
    outs[0][2 : 2 + shared.shape[0], :] = shared
    outs[0][2 + shared.shape[0] :, :] = jnp.zeros((SMALL - 2 - shared.shape[0], expand.shape[1]), F32)


def blocks_body(block, here, ins, outs):
    *terms, small, small_got = ins
    (out,) = outs
    low = (small[...] + small_got[...]).astype(BF)
    tall = block + SMALL
    for j in range(out.shape[0] // tall):
        rows = slice(j * block, (j + 1) * block)
        out[j * tall : j * tall + block, :] = sum(term[rows, :].astype(F32) for term in terms).astype(BF)
        out[j * tall + block : (j + 1) * tall, :] = low


def heads_body(part, here, ins, outs):
    (parts,) = ins
    g_query, g_key, g_value, g_output, small = outs
    block = g_query.shape[0]
    tall = block + SMALL
    count = parts.shape[0] // tall
    low = sum(parts[j * tall + block : (j + 1) * tall, :].astype(F32) for j in range(count))
    small[...] = low
    small.send()
    sums = sum(parts[j * tall : j * tall + block, :].astype(F32) for j in range(count))
    for i, out in enumerate((g_query, g_key, g_value)):
        out[...] = sums[:, i * part : (i + 1) * part]
        out.send()
    g_output[...] = sums[:, 3 * part :].T


def feeds_body(here, ins, outs):
    expand_a, expand_b, reduce_a, reduce_b = ins
    g_expand, g_reduce = outs
    g_expand[...] = expand_a[...].astype(F32) + expand_b[...].astype(F32)
    g_expand.send()
    g_reduce[...] = (reduce_a[...].astype(F32) + reduce_b[...].astype(F32)).T


def spread_body(*refs):
    ins, out, buffer, in_sems, out_sems = refs[:4], refs[4], refs[5], refs[6], refs[7]
    strip = lax.axis_index("mp")
    reads = [pltpu.make_async_copy(ins[s], buffer.at[s], in_sems.at[s]) for s in range(4)]
    writes = [pltpu.make_async_copy(buffer.at[s], out.at[strip ^ s], out_sems.at[s]) for s in range(4)]
    for read in reads:
        read.start()
    for read, write in zip(reads, writes):
        read.wait()
        write.start()
    for write in writes:
        write.wait()


def spread(strips):
    rows, width = strips[0].shape
    dtype = strips[0].dtype
    return pl.pallas_call(
        spread_body,
        in_specs=[ANY] * 4,
        out_specs=ANY,
        out_shape=shape((4, rows, width), dtype),
        scratch_shapes=[pltpu.VMEM((4, rows, width), dtype)] + [pltpu.SemaphoreType.DMA((4,))] * 2,
        cost_estimate=pl.CostEstimate(flops=0, bytes_accessed=16 * rows * width, transcendentals=0),
    )(*strips)


def swap(values, axis, size, bit):
    return lax.ppermute(values, axis, [(i, i ^ (1 << bit)) for i in range(size)])


def tie(*values):
    return lax.optimization_barrier(values)


def plain_sums(part, feeds, heads, small):
    def scattered(values):
        total = sum(v.astype(F32) for v in values)
        return lax.psum_scatter(total, "dp", scatter_dimension=0, tiled=True)

    g_expand, g_reduce = (scattered([v[i] for v in feeds]) for i in range(2))
    total = scattered(heads)
    g_query, g_key, g_value = (total[:, i * part : (i + 1) * part] for i in range(3))
    small = jnp.concatenate(small_total(*lax.psum((small, *others(small)), "dp")))
    return g_query, g_key, g_value, total[:, 3 * part :].T, g_expand, g_reduce.T, small


def others(small):
    return [lax.ppermute(small, "mp", [(i, i ^ k) for i in range(4)]) for k in (1, 2, 3)]


def total_of(*values):
    return sum(v.astype(F32) for v in values).astype(BF)


def arranged(result, grad_tokens, part, g_query, g_key, g_value, g_output, g_expand, g_reduce, small):
    b_reduce, b_output, gain_two, shift_two, gain_one, shift_one = (small[i] for i in range(2, 8))
    return (
        result,
        grad_tokens,
        g_query,
        small[1, :part],
        g_key,
        g_value,
        small[1, part : 2 * part],
        g_output,
        b_output,
        g_expand,
        small[0],
        g_reduce,
        b_reduce,
        gain_one,
        shift_one,
        gain_two,
        shift_two,
    )


def local(
    sizes,
    tokens,
    visible,
    w_query,
    b_query,
    w_key,
    w_value,
    b_value,
    w_output,
    b_output,
    w_expand,
    b_expand,
    w_reduce,
    b_reduce,
    gain_first,
    shift_first,
    gain_second,
    shift_second,
    cotangent,
):
    n_dp, n_mp = sizes
    part, units, (_, rows, width) = w_query.shape[1], w_expand.shape[1], tokens.shape
    core = partial(swap, axis="mp", size=n_mp, bit=0)
    across = partial(swap, axis="mp", size=n_mp, bit=1)
    over = [partial(swap, axis="dp", size=n_dp, bit=b) for b in range(n_dp.bit_length() - 1)]
    flat, tall, moved = Held((rows, width), BF), Held((width, rows), BF), shape((rows, width), BF)
    wide, rows8, rows16 = Held((rows, width), F32), Held((8, width), F32), shape((SMALL, width), F32)
    flop = 2 * rows * width * width
    block = width // n_dp
    halving = n_dp == 8 and block % 16 == 0

    third = 4 * part // 3
    direct, first, pack0, small0 = run(
        pack_body,
        (
            stacked(w_query.T, w_key.T, w_value.T, w_output, fixed=True),
            *(
                Arg([v], v.shape, fixed=True)
                for v in (
                    b_query,
                    b_value,
                    b_expand,
                    gain_first,
                    shift_first,
                    gain_second,
                    shift_second,
                    b_output,
                    b_reduce,
                )
            ),
        ),
        [
            shape((third, width), BF),
            shape((SMALL + third, width), BF),
            shape((4 * part, width), BF),
            shape((SMALL, width), BF),
        ],
        1000,
    )
    direct, first, pack1, small1 = across(direct), across(first), core(pack0), core(small0)
    n1, n1t = run(first_norm, (own(tokens), small0), (flat, tall), flop // 100)
    n1, pack1, small1 = tie(n1, pack1, small1)
    near = run(near_attention, (held(n1), small0, pack0, small1, pack1), heads_shapes(rows, part, 2), 2 * flop, visible)
    *near, n1, direct, w_exp, w_red, cot = tie(*near, n1, direct, w_expand, w_reduce, cotangent)
    relayed, direct3 = over[0](direct), core(direct)
    exp1, red1 = core(w_exp), core(w_red)
    exp1, red1 = tie(exp1, red1)
    branch, branch_t, cross, cross_t, d_reduce, *d_hidden = run(
        branch_of,
        (own(cot), other(cot), held(w_red), held(red1)),
        (flat, tall, flat, tall, rows8, *[flat] * 4),
        flop // 100,
        visible,
    )
    branch, first, relayed = tie(branch, first, relayed)
    pack2, pack3 = (first, direct, relayed), (core(first), direct3, core(relayed))
    *pack3, branch, n1 = tie(*pack3, branch, n1)
    small2, small3 = rows_of(pack2[0], 0, SMALL), rows_of(pack3[0], 0, SMALL)
    pack2, pack3 = pieced(*pack2), pieced(*pack3)
    half, half_t = Held((rows // 2, width), BF), Held((width, rows // 2), BF)
    half_moved = shape((rows // 2, width), BF)
    *away, resid, n2, n2t, n2a, n2b = run(
        far_attention,
        (
            held(n1),
            small2,
            pack2,
            small3,
            pack3,
            held(near[5]),
            rows_of(pack0, 3 * part, part),
            rows_of(pack1, 3 * part, part),
            own(tokens),
            small0,
        ),
        [*heads_shapes(rows, part, 2), wide, flat, tall, half_moved, half_moved],
        3 * flop,
        visible,
    )
    n2a, n2b = across(n2a), across(n2b)
    grads = shape((2, width, units), BF)
    g0, g1, de_near, mlp, dn2 = run(
        near_feed,
        (
            *map(held, (n2, exp1, w_exp, red1, w_red, d_hidden[1], d_hidden[0], n2t, branch_t)),
            small1,
            small0,
        ),
        [grads, grads, rows8, wide, wide],
        12 * flop,
    )

    def cross_half(normed, first):
        gradients = [held(v, first, rows // 2) for v in (d_hidden[3], d_hidden[2])]
        return run(
            cross_feed,
            (normed, held(exp1), held(w_exp), *gradients, small1, small0),
            [half, half, half, half, half_t, half_moved],
            3 * flop,
        )

    g0, g1, n2a = tie(g0, g1, n2a)
    *half_a, dn2_back = cross_half(n2a, 0)
    got_a = across(dn2_back)
    half_a[0], n2b = tie(half_a[0], n2b)
    *half_b, dn2_back = cross_half(n2b, rows // 2)
    got_b = across(dn2_back)
    near_a, near_b = ([held(v) for v in (h[0], h[1], h[4])] for h in (half_a, half_b))
    g1, de_one = run(
        cross_one, (held(cross_t), g1, held(de_near), *near_a, *near_b), [grads, rows8], 2 * flop
    )
    g1, de_one, got_a = tie(g1, de_one, got_a)
    got0 = core(g1)
    near_a, near_b = ([held(v) for v in (h[0], h[2], h[3], h[4])] for h in (half_a, half_b))
    de_near, g1 = tie(de_near, g1)
    g0, de_zero, mlp_back = run(
        cross_zero,
        (held(cross_t), g0, *map(held, (de_near, red1, w_red)), *near_a, *near_b),
        [grads, rows8, moved],
        4 * flop,
    )
    if halving:
        g0, got0, mlp_back = tie(g0, got0, mlp_back)
    mlp_got = across(mlp_back)
    if halving:
        (pay_x, pay_z), (kept_e, kept_r), _ = stage(
            [
                ("halve", (entry(g0, 0), entry(got0, 0)), 0, 0, block),
                ("halve", (entry(g0, 1), entry(got0, 1)), 1, 1, 2 * block),
            ],
            width,
        )
        got_e, got_r = over[0](pay_x), over[1](pay_z)
        got_b, kept_e = tie(got_b, kept_e)
    grads = shape((width, 4 * part), BF)
    extra = (pltpu.VMEM((rows, 3 * part), BF), pltpu.VMEM((1, width), F32))

    def saved_of(saved, s):
        n = part // HD
        return [held(a, s * n, n) for a in saved[:5]] + [held(saved[5])]

    h2, h3, ds_far, dn1, grad_resid, attn, attn_t, sums2 = run(
        far_back,
        (
            held(resid),
            held(dn2),
            stacked(got_a, got_b),
            held(branch),
            small0,
            pack3,
            held(n1t),
            *map(held, away),
            pack2,
        ),
        [grads, grads, rows8, wide, wide, flat, tall, rows8],
        8 * flop,
        scratch=extra,
    )
    if halving:
        h2, h3, attn, mlp_got, got_e, got_r, kept_e = tie(h2, h3, attn, mlp_got, got_e, got_r, kept_e)
    got_h2 = core(h3)

    def back(column, attn, pack, saved, d_norm):
        return run(
            partial(slot_back, column),
            (held(attn), pack, held(attn_t), held(n1t), *saved_of(saved, column), held(d_norm)),
            [*[shape((width // 2, 4 * part), BF)] * 2, rows8, wide],
            4 * flop,
            scratch=extra,
        )

    h2, mlp_got = tie(h2, mlp_got)
    (result,) = run(
        result_body, (held(resid), held(mlp), mlp_got, small0), [shape((rows, width), BF)], flop // 100, visible
    )
    if halving:
        result_far, result_near = across(result), core(result)
        result, h2, got_h2, attn = tie(result, h2, got_h2, attn)
        (pay_z, pay_x, pay_h), (kept_e, kept_r, kept_h), _ = stage(
            [
                ("halve", (held(kept_e), got_e), 0, 1, block),
                ("halve", (held(kept_r), got_r), 1, 0, block),
                ("halve", (h2, got_h2), 2, 0, block),
            ],
            width,
        )
        got_z, got_x, got_h = over[1](pay_z), over[0](pay_x), over[0](pay_h)
        attn, kept_e, result_near = tie(attn, kept_e, result_near)
    *h1, ds1, dn1 = back(1, attn, pack1, near, dn1)
    if halving:
        attn, got_z, got_x, kept_e, *h1 = tie(attn, got_z, got_x, kept_e, *h1)
    got_h0 = [core(v) for v in h1]
    if halving:
        (pay_w,), (kept_e, kept_r), places_w = stage(
            [("halve", (held(kept_e), got_z), 0, 2, block), ("halve", (held(kept_r), got_x), 0, 2, block)], width
        )
        got_w = over[2](pay_w)
        attn, kept_e = tie(attn, kept_e)
    h0, strip, small = run(
        last_back,
        (
            held(attn),
            pack0,
            held(attn_t),
            held(n1t),
            *saved_of(near, 0),
            held(dn1),
            own(tokens),
            held(grad_resid),
            small0,
            *map(held, (de_zero, de_one, ds_far, ds1, d_reduce, sums2)),
        ),
        [grads, shape((rows, width), BF), rows16],
        4 * flop,
        scratch=extra,
    )
    if not halving:
        grad_tokens, result = (spread([v, core(v), across(v), core(across(v))]) for v in (strip, result))
        heads_got = across(total_of(h2, got_h2))
        sums = plain_sums(part, (g0, got0), (h0, jnp.concatenate(got_h0), heads_got), small)
        return arranged(result, grad_tokens, part, *sums)
    h0, strip, small, got_h, result_far, *got_h0 = tie(h0, strip, small, got_h, result_far, *got_h0)
    (pay_y, pay_x), (kept_h0,), _ = stage(
        [("sum", (held(kept_h), got_h), 0), ("halve", (h0, stacked(*got_h0)), 1, 0, block)], width
    )
    got_h0, heads_got = over[0](pay_x), across(pay_y)
    kept_h0, small = tie(kept_h0, small)
    small_got = others(small)
    kept_h0, strip, got_w, *small_got = tie(kept_h0, strip, got_w, *small_got)
    (small,) = run(small_body, (small, *small_got), [rows16], 1000)
    small_got = over[0](small)
    strip_far, strip_near, result_diag = across(strip), core(strip), core(result_far)
    small, kept_h0, result, result_diag = tie(small, kept_h0, result, result_diag)
    first_w, second_w = (rows_of(got_w, place[1], place[2]) for place in places_w)
    g_expand, g_reduce = run(
        feeds_body,
        (held(kept_e), first_w, held(kept_r), second_w),
        [shape((block, units), F32), shape((units, block), F32)],
        1000,
    )
    result = spread([result, result_near, result_far, result_diag])
    result, g_expand, kept_h0, got_h0, heads_got, small_got = tie(
        result, g_expand, kept_h0, got_h0, heads_got, small_got
    )
    column = n_dp // 2
    (sums,) = run(
        partial(blocks_body, block),
        (held(kept_h0), got_h0, heads_got, small, small_got),
        [shape((column * (block + SMALL), width), BF)],
        1000,
    )
    columns = [[2 * z + x for z in range(column)] for x in range(2)]
    sums_got = lax.all_to_all(sums, "dp", 0, 0, axis_index_groups=columns, tiled=True)
    sums, strip_far = tie(sums, strip_far)
    strip_diag = core(strip_far)
    sums, strip_diag = tie(sums, strip_diag)
    grad_tokens = spread([strip, strip_near, strip_far, strip_diag])
    grad_tokens, sums_got = tie(grad_tokens, sums_got)
    narrow, thin = shape((block, part), F32), shape((part, block), F32)
    *heads, small = run(partial(heads_body, part), (sums_got,), [narrow, narrow, narrow, thin, rows16], 1000)
    return arranged(result, grad_tokens, part, *heads, g_expand, g_reduce, small)


def solution(mesh):
    placed = (
        P("dp", None, None),
        P("dp"),
        P(None, "mp"),
        P("mp"),
        P(None, "mp"),
        P(None, "mp"),
        P("mp"),
        P("mp", None),
        P(),
        P(None, "mp"),
        P("mp"),
        P("mp", None),
        P(),
        P(),
        P(),
        P(),
        P(),
        P("dp", None, None),
    )
    return jax.shard_map(
        partial(local, (mesh.shape["dp"], mesh.shape["mp"])),
        mesh=mesh,
        in_specs=placed,
        out_specs=(
            P("dp", None, None),
            P("dp", None, None),
            P("dp", "mp"),
            P("mp"),
            P("dp", "mp"),
            P("dp", "mp"),
            P("mp"),
            P("mp", "dp"),
            P(),
            P("dp", "mp"),
            P("mp"),
            P("mp", "dp"),
            P(),
            P(),
            P(),
            P(),
            P(),
        ),
        check_vma=False,
    )
```

```python
from functools import partial

import jax
import jax.numpy as jnp
from jax import lax
from jax.experimental import pallas as pl
from jax.experimental.pallas import tpu as pltpu
from jax.sharding import PartitionSpec as P

HD = 64
F32 = jnp.float32
BF = jnp.bfloat16
NT = (((1,), (1,)), ((), ()))
ANY = pl.BlockSpec(memory_space=pl.ANY)
SMEM = pl.BlockSpec(memory_space=pltpu.SMEM)
VMEM = pl.BlockSpec(memory_space=pltpu.VMEM)


def dot(left, right):
    return jnp.dot(left, right, preferred_element_type=F32)


def dot_nt(left, right):
    return lax.dot_general(left, right, NT, preferred_element_type=F32)


def shape(dims, dtype):
    return jax.ShapeDtypeStruct(dims, dtype)


class Load:
    def __init__(self, buffer, copies=()):
        self.buffer, self.copies = buffer, copies
        for copy in copies:
            copy.start()

    def ref(self):
        for copy in self.copies:
            copy.wait()
        self.copies = ()
        return self.buffer

    def __getitem__(self, index):
        return self.ref()[index]

    @property
    def shape(self):
        return self.buffer.shape


class Store:
    def __init__(self, buffer, target=None, sems=None):
        self.target, self.buffer, self.sems = target, buffer, sems
        self.copies = []

    def start(self, source, target):
        self.copies.append(pltpu.make_async_copy(source, target, self.sems.at[len(self.copies)]))
        self.copies[-1].start()

    def send(self, *index):
        if self.target is not None:
            self.start(*((self.buffer.at[index], self.target.at[index]) if index else (self.buffer, self.target)))

    def send_from(self, view):
        self.start(view, self.target)

    def close(self):
        if not self.copies:
            self.send()
        for copy in self.copies:
            copy.wait()

    def __setitem__(self, index, value):
        self.buffer[index] = value

    def __getitem__(self, index):
        return self.buffer[index]

    @property
    def shape(self):
        return self.buffer.shape


class Held:
    def __init__(self, dims, dtype):
        self.struct = shape(dims, dtype)


PIECES = 8
SMALL = 16


class Arg:
    def __init__(self, arrays, dims, view=None, offset=None, counts=None, held=False, firsts=None, fixed=False):
        self.arrays, self.dims, self.view, self.offset, self.held = arrays, dims, view, offset, held
        self.fixed = fixed
        self.firsts = firsts or [0] * len(arrays)
        self.counts = counts or [a.shape[0] for a in arrays]


def own(array):
    return Arg([array], array.shape[1:], view=lambda ref, here: ref.at[here["strip"]], fixed=True)


def other(array):
    return Arg([array], array.shape[1:], view=lambda ref, here: ref.at[here["strip"] ^ 2], fixed=True)


def entry(array, index):
    return Arg([array], array.shape[1:], view=lambda ref, here: ref.at[index])


def held(array, first=None, count=None):
    if first is None:
        return Arg([array], array.shape, held=True)
    view = lambda ref, here: ref.at[pl.ds(first, count)]
    return Arg([array], (count, *array.shape[1:]), view=view, held=True)


def rows_of(array, first, count):
    return Arg([array], (count, *array.shape[1:]), view=lambda ref, here: ref.at[pl.ds(first, count)])


def stacked(*arrays, counts=None, fixed=False):
    counts = counts or [a.shape[0] for a in arrays]
    starts = [sum(counts[:i]) for i in range(len(counts))]
    dims = (sum(counts), arrays[0].shape[1])
    return Arg(list(arrays), dims, offset=lambda here: starts, counts=counts, fixed=fixed)


def pieced(first, direct, relayed):
    base, count = first.shape[0], direct.shape[0]

    def offset(here):
        bit = here["bit"]
        return (
            0,
            pl.multiple_of(base + count * bit, 16),
            pl.multiple_of(base + count * (1 - bit), 16),
        )

    return Arg([first, direct, relayed], (base + 2 * count, first.shape[1]), offset=offset)


LIMIT = 17


def run(body, args, outs, flops, visible=None, scratch=()):
    args = [a if isinstance(a, Arg) else Arg([a], a.shape) for a in args]
    arrays = [array for a in args for array in a.arrays]
    loaded = [a for a in args if not a.held]
    stay = [isinstance(o, Held) for o in outs]
    structs = [o.struct if isinstance(o, Held) else o for o in outs]
    n_arrays, n_out, n_stored = len(arrays), len(outs), len(outs) - sum(stay)

    def kernel(*refs):
        here = {"strip": lax.axis_index("mp"), "bit": lax.axis_index("dp") & 1, "dp": lax.axis_index("dp")}
        if visible is not None:
            visible_ref, *refs = refs
            here["visible"] = visible_ref[here["strip"]]
            here["visible_across"] = visible_ref[here["strip"] ^ 2]
        ins, results, refs = refs[:n_arrays], refs[n_arrays : n_arrays + n_out], refs[n_arrays + n_out :]
        in_buffers, refs = list(refs[: len(loaded)]), refs[len(loaded) :]
        out_buffers, (in_sems, out_sems, *rest) = list(refs[:n_stored]), refs[n_stored:]
        loads, j = [], 0
        for a in args:
            if a.held:
                loads.append(Load(ins[j] if a.view is None else a.view(ins[j], here)))
                j += 1
                continue
            buffer, copies = in_buffers.pop(0), []
            offsets = a.offset(here) if a.offset is not None else None
            for i, array in enumerate(a.arrays):
                source = a.view(ins[j], here) if a.view is not None else ins[j]
                target = buffer if offsets is None else buffer.at[pl.ds(offsets[i], a.counts[i])]
                if offsets is not None and a.counts[i] < array.shape[0]:
                    source = source.at[pl.ds(a.firsts[i], a.counts[i])]
                copies.append(pltpu.make_async_copy(source, target, in_sems.at[j]))
                j += 1
            loads.append(Load(buffer, copies))
        stores = []
        for i, (result, stays) in enumerate(zip(results, stay)):
            stores.append(Store(result) if stays else Store(out_buffers.pop(0), result, out_sems.at[i]))
        body(here, loads, stores, *rest)
        for load in loads:
            load.ref()
        for store in stores:
            store.close()

    moved = sum(a.size * a.dtype.itemsize for a in [*arrays, *structs])
    scratches = [pltpu.VMEM(a.dims, a.arrays[0].dtype) for a in loaded]
    scratches += [pltpu.VMEM(o.shape, o.dtype) for o, stays in zip(structs, stay) if not stays]
    scratches += [pltpu.SemaphoreType.DMA((n_arrays,)), pltpu.SemaphoreType.DMA((n_out, PIECES))]
    return pl.pallas_call(
        kernel,
        in_specs=[SMEM] * (visible is not None) + [VMEM if a.held else ANY for a in args for _ in a.arrays],
        out_specs=tuple(VMEM if stays else ANY for stays in stay),
        out_shape=tuple(structs),
        scratch_shapes=scratches + list(scratch),
        cost_estimate=pl.CostEstimate(flops=flops, bytes_accessed=moved, transcendentals=0),
        compiler_params=pltpu.CompilerParams(vmem_limit_bytes=LIMIT << 20),
    )(
        *([] if visible is None else [visible]),
        *(
            pltpu.with_memory_space_constraint(array, pltpu.HBM) if a.fixed else array
            for a in args
            for array in a.arrays
        ),
    )


def norm_parts(values):
    center = values - jnp.mean(values, axis=-1, keepdims=True)
    rstd = lax.rsqrt(jnp.mean(center * center, axis=-1, keepdims=True) + 1e-06)
    return center * rstd, rstd


def norm_back(unit, rstd, gain, grad):
    scaled = grad * gain
    first = jnp.mean(scaled, axis=-1, keepdims=True)
    second = jnp.mean(scaled * unit, axis=-1, keepdims=True)
    return rstd * (scaled - first - unit * second)


def row_sum(values):
    return jnp.sum(values, axis=0, keepdims=True)


BIAS_EXPAND, BIAS_HEADS, GAIN_ONE, SHIFT_ONE, GAIN_TWO, SHIFT_TWO, BIAS_OUT, BIAS_REDUCE = range(8)


def vector(vectors, row):
    return vectors[row : row + 1, :].astype(F32)


def pack_body(here, ins, outs):
    pieces, b_query, b_value, *vectors = ins
    choice, first, pack, small = outs
    rows = pieces.ref()
    third = choice.shape[0]
    choice.send_from(rows.at[pl.ds(pl.multiple_of(third * (1 + here["bit"]), 16), third)])
    first.start(rows.at[pl.ds(0, third)], first.target.at[pl.ds(SMALL, third)])
    pack.send_from(rows)
    small[...] = jnp.zeros(small.shape, BF)
    part = b_query.shape[0]
    small[BIAS_HEADS : BIAS_HEADS + 1, :part] = b_query[...].reshape(1, part)
    small[BIAS_HEADS : BIAS_HEADS + 1, part : 2 * part] = b_value[...].reshape(1, part)
    rows_of_vectors = (BIAS_EXPAND, GAIN_ONE, SHIFT_ONE, GAIN_TWO, SHIFT_TWO, BIAS_OUT, BIAS_REDUCE)
    for row, values in zip(rows_of_vectors, vectors):
        small[row : row + 1, :] = values[...].reshape(1, values.shape[0])
    first.start(small.buffer, first.target.at[pl.ds(0, SMALL)])
    small.send()


def first_norm(here, ins, outs):
    tok, vectors = ins
    normed, normed_t = outs
    unit, _ = norm_parts(tok[...].astype(F32))
    low = (unit * vector(vectors, GAIN_ONE) + vector(vectors, SHIFT_ONE)).astype(BF)
    normed[...] = low
    normed_t[...] = low.T


def branch_of(here, ins, outs):
    cot, cross, red0, red1 = ins
    total, hidden = outs[4], outs[5:]
    for i, (strip, name) in enumerate(((cot, "visible"), (cross, "visible_across"))):
        branch, branch_t = outs[2 * i : 2 * i + 2]
        row = lax.broadcasted_iota(jnp.int32, strip.shape, 0)
        kept = jnp.where(row < here[name], strip[...].astype(F32), 0.0)
        low = kept.astype(BF)
        branch[...] = low
        branch_t[...] = low.T
        hidden[2 * i][...] = dot_nt(low, red0[...]).astype(BF)
        hidden[2 * i + 1][...] = dot_nt(low, red1[...]).astype(BF)
        if i == 0:
            total[...] = jnp.broadcast_to(row_sum(kept), total.shape)


def heads_forward(here, normed, smalls, packs, outs):
    q_out, k_out, v_out, e_out, o_out, ctx_out = outs
    rows, width = normed.shape
    part = width // 4
    heads = part // HD
    lane = lax.broadcasted_iota(jnp.int32, (rows, HD), 1)
    row = lax.broadcasted_iota(jnp.int32, (rows, HD), 0)
    one = jnp.where(lane == 0, 1.0, 0.0).astype(BF)
    mask = jnp.where((lane == 0) & (row >= here["visible"]), -1e30, 0.0).astype(BF)
    low = normed[...]
    for s, pack in enumerate(packs):
        biases = vector(smalls[s], BIAS_HEADS)
        at = pack.shape[0] - 4 * part
        rows_q, rows_k, rows_v = (slice(at + i * part, at + (i + 1) * part) for i in range(3))
        q = (dot_nt(low, pack[rows_q, :]) + biases[:, :part]).astype(BF) * BF(HD**-0.5)
        k = dot_nt(low, pack[rows_k, :]).astype(BF)
        v = (dot_nt(low, pack[rows_v, :]) + biases[:, part : 2 * part]).astype(BF)
        for h in range(heads):
            cols = slice(h * HD, (h + 1) * HD)
            i = s * heads + h
            q_out[i, :, :HD] = q[:, cols]
            q_out[i, :, HD:] = one
            k_out[i, :, :HD] = k[:, cols]
            k_out[i, :, HD:] = mask
            v_out[i, :, :HD] = v[:, cols]
            v_out[i, :, HD:] = one
    for out in (q_out, k_out, v_out):
        out.send()
    for i in range(len(packs) * heads):
        scores = dot_nt(q_out[i], k_out[i])
        e = jnp.exp(scores - jnp.max(scores, axis=1, keepdims=True)).astype(BF)
        e_out[i] = e
        e_out.send(i)
        o = dot(e, v_out[i])
        o_out[i] = o
        ctx_out[:, i * HD : (i + 1) * HD] = (o[:, :HD] * (1.0 / o[:, HD : HD + 1])).astype(BF)
    o_out.send()
    ctx_out.send()


def heads_shapes(rows, part, slots):
    n = slots * part // HD
    outs = [Held((n, rows, 2 * HD), BF)] * 3
    return outs + [Held((n, rows, rows), BF), Held((n, rows, 2 * HD), F32), Held((rows, n * HD), BF)]


def near_attention(here, ins, outs):
    normed, small0, pack0, small1, pack1 = ins
    heads_forward(here, normed, (small0, small1), (pack0, pack1), outs)


def far_attention(here, ins, outs):
    normed, small2, pack2, small3, pack3, ctx, wo0, wo1, tok, vectors = ins
    heads_forward(here, normed, (small2, small3), (pack2, pack3), outs[:6])
    resid, normed_two, normed_two_t, *halves = outs[6:]
    part = wo0.shape[0]
    total = tok[...].astype(F32) + vector(vectors, BIAS_OUT)
    total += dot(ctx[:, :part], wo0[...]) + dot(ctx[:, part:], wo1[...])
    far = outs[5]
    total += dot(far[:, :part], pack2[-part:, :])
    total += dot(far[:, part:], pack3[-part:, :])
    resid[...] = total
    resid.send()
    unit, _ = norm_parts(total)
    low = (unit * vector(vectors, GAIN_TWO) + vector(vectors, SHIFT_TWO)).astype(BF)
    normed_two[...] = low
    count = halves[0].shape[0]
    for i, half in enumerate(halves):
        half.send_from(normed_two.buffer.at[pl.ds(i * count, count)])
    normed_two_t[...] = low.T


def hidden_of(normed, d_hidden, small, we):
    pre = dot(normed[...], we[...]) + vector(small, BIAS_EXPAND)
    cdf = 0.5 * (1.0 + lax.erf(pre * 0.7071067811865476))
    slope = cdf + pre * (jnp.exp(-0.5 * pre * pre) * 0.3989422804014327)
    return (pre * cdf).astype(BF), (d_hidden[...].astype(F32) * slope).astype(BF)


def near_feed(here, ins, outs):
    normed, exp1, exp0, red1, red0, d_hidden1, d_hidden0, normed_t, branch_t, small1, small0 = ins
    grad0, grad1, d_small, mlp, d_norm = outs
    total, back = None, None
    for s, (grads, we, wr, d_hidden, small) in enumerate(
        ((grad1, exp1, red1, d_hidden1, small1), (grad0, exp0, red0, d_hidden0, small0))
    ):
        hidden, d_pre = hidden_of(normed, d_hidden, small, we)
        grads[0] = dot(normed_t[...], d_pre).astype(BF)
        grads.send(0)
        grads[1] = dot(branch_t[...], hidden).astype(BF)
        grads.send(1)
        d_small[s : s + 1, :] = row_sum(d_pre.astype(F32))
        out = dot(hidden, wr[...])
        total = out if total is None else total + out
        out = dot_nt(d_pre, we[...])
        back = out if back is None else back + out
    mlp[...], d_norm[...] = total, back


def cross_feed(here, ins, outs):
    normed, exp1, exp0, d_hidden1, d_hidden0, small1, small0 = ins
    hidden1, d_pre1, hidden0, d_pre0, normed_t, d_norm = outs
    h, d = hidden_of(normed, d_hidden1, small1, exp1)
    hidden1[...], d_pre1[...] = h, d
    back = dot_nt(d, exp1[...])
    h, d = hidden_of(normed, d_hidden0, small0, exp0)
    hidden0[...], d_pre0[...] = h, d
    normed_t[...] = normed[...].T
    d_norm[...] = (back + dot_nt(d, exp0[...])).astype(BF)


def cross_slot(grads, d_small, cross_t, part, d_near, halves, hidden, d_pre):
    rows = halves[0][0].shape[0]

    def over_halves(left, right):
        return sum(dot(left(i), right(i)) for i in range(2))

    grads[1] = (
        over_halves(lambda i: cross_t[:, i * rows : (i + 1) * rows], lambda i: halves[i][hidden][...])
        + part[1].astype(F32)
    ).astype(BF)
    grads.send(1)
    grads[0] = (
        over_halves(lambda i: halves[i][-1][...], lambda i: halves[i][d_pre][...]) + part[0].astype(F32)
    ).astype(BF)
    grads.send(0)
    d_small[0:1, :] = d_near + sum(row_sum(halves[i][d_pre][...].astype(F32)) for i in range(2))


def cross_one(here, ins, outs):
    cross_t, part, d_near, *halves = ins
    count = len(halves) // 2
    cross_slot(outs[0], outs[1], cross_t, part, d_near[0:1, :], (halves[:count], halves[count:]), 0, 1)


def cross_zero(here, ins, outs):
    cross_t, part, d_near, red1, red0, *halves = ins
    grads, d_small, mlp = outs
    count = len(halves) // 2
    halves = halves[:count], halves[count:]
    rows = halves[0][0].shape[0]
    cross_slot(grads, d_small, cross_t, part, d_near[1:2, :], halves, 1, 2)
    for i in range(2):
        out = dot(halves[i][0][...], red1[...]) + dot(halves[i][1][...], red0[...])
        mlp[i * rows : (i + 1) * rows, :] = out.astype(BF)


def heads_backward(attn, attn_t, normed_t, saved, s, column, pack, grads, d_small, d_in):
    q_in, k_in, v_in, e_in, o_in, ctx = saved
    part = ctx.shape[1] // 2
    at_pack = pack.shape[0] - 4 * part
    heads = part // HD
    d_ctx = dot_nt(attn[...], pack[at_pack + 3 * part :, :]).astype(BF).astype(F32)
    back_v, back_k = [], []
    for h in range(s * heads, (s + 1) * heads):
        o = o_in[h]
        inverse = 1.0 / o[:, HD : HD + 1]
        at = h - s * heads
        do = (d_ctx[:, at * HD : (at + 1) * HD] * inverse).astype(BF)
        term = jnp.sum(do.astype(F32) * o[:, :HD], axis=1, keepdims=True) * inverse
        e = e_in[h]
        d_prob = dot_nt(do, v_in[h][:, :HD])
        d_score = (e.astype(F32) * (d_prob - term)).astype(BF)
        back_v.append(dot(do.T, e))
        back_k.append(dot(q_in[h][:, :HD].T, d_score))
        d_in[:, at * HD : (at + 1) * HD] = (dot(d_score, k_in[h][:, :HD]) * HD**-0.5).astype(BF)
    d_in[:, part : 2 * part] = jnp.concatenate(back_k, axis=0).T.astype(BF)
    d_in[:, 2 * part :] = jnp.concatenate(back_v, axis=0).T.astype(BF)
    grads[:, : 3 * part] = dot(normed_t[...], d_in[...]).astype(BF)
    grads[:, 3 * part :] = dot(attn_t[...], ctx[:, column * part : (column + 1) * part]).astype(BF)
    grads.send()
    d_small[:, :part] = row_sum(d_in[:, :part].astype(F32))
    d_small[:, part : 2 * part] = row_sum(d_in[:, 2 * part :].astype(F32))
    return dot(d_in[...], pack[at_pack : at_pack + 3 * part, :])


def far_back(here, ins, outs, d_in, d_row):
    resid, d_norm, got, branch, vectors, pack3, normed_t, *saved, pack2 = ins
    grad2, grad3, d_small, out, grad, attn, attn_t, sums = outs
    unit, rstd = norm_parts(resid[...])
    dn = d_norm[...] + got[...].astype(F32)
    g = branch[...].astype(F32) + norm_back(unit, rstd, vector(vectors, GAIN_TWO), dn)
    grad[...] = g
    grad.send()
    low = g.astype(BF)
    attn[...] = low
    attn.send()
    attn_t[...] = low.T
    attn_t.send()
    sums[0:1, :] = row_sum(low.astype(F32))
    sums[1:2, :] = row_sum(dn * unit)
    sums[2:3, :] = row_sum(dn)
    d_row[...] = jnp.zeros(d_row.shape, F32)
    back = heads_backward(attn, attn_t, normed_t, saved, 1, 1, pack3, grad3, d_row, d_in)
    d_small[0:1, :] = d_row[...]
    back = back + heads_backward(attn, attn_t, normed_t, saved, 0, 0, pack2, grad2, d_row, d_in)
    d_small[1:2, :] = d_row[...]
    out[...] = back


def result_body(here, ins, outs):
    resid, mlp, got, vectors = ins
    row = lax.broadcasted_iota(jnp.int32, resid.shape, 0)
    total = resid[...] + (mlp[...] + got[...].astype(F32) + vector(vectors, BIAS_REDUCE))
    outs[0][...] = jnp.where(row < here["visible"], total, 0.0).astype(BF)


class Rows:
    def __init__(self, parts):
        self.parts = parts

    def __setitem__(self, index, value):
        rows, columns = index
        start = 0
        for part in self.parts:
            count = part.shape[0]
            part[:, columns] = value[start : start + count, :]
            start += count

    def send(self):
        for part in self.parts:
            part.send()


def slot_back(column, here, ins, outs, d_in, d_row):
    attn, pack, attn_t, normed_t, *saved, d_norm = ins
    grads, (d_small, out) = Rows(outs[:-2]), outs[-2:]
    d_row[...] = jnp.zeros(d_row.shape, F32)
    dn = heads_backward(attn, attn_t, normed_t, saved, 0, column, pack, grads, d_row, d_in)
    d_small[0:1, :] = d_row[...]
    out[...] = d_norm[...] + dn


def last_back(here, ins, outs, d_in, d_row):
    attn, pack, attn_t, normed_t, *rest = ins
    saved, (d_norm, tok, grad, vectors, *small) = rest[:6], rest[6:]
    grads, out, small_out = outs
    d_row[...] = jnp.zeros(d_row.shape, F32)
    dn = d_norm[...] + heads_backward(
        attn, attn_t, normed_t, saved, 0, 0, pack, grads, d_row, d_in
    )
    unit, rstd = norm_parts(tok[...].astype(F32))
    out[...] = (grad[...] + norm_back(unit, rstd, vector(vectors, GAIN_ONE), dn)).astype(BF)
    out.send()
    feed0, feed1, d_far, d_one, d_reduce, sums = small
    small_out[...] = jnp.zeros(small_out.shape, F32)
    late = [feed0[0:1, :], d_row[...], feed1[0:1, :], d_one[0:1, :], d_far[1:2, :], d_far[0:1, :]]
    late += [d_reduce[0:1, :], sums[0:3, :], row_sum(dn * unit), row_sum(dn)]
    start = 0
    for values in late:
        small_out[start : start + values.shape[0], :] = values
        start += values.shape[0]


def stage_body(items, counts, here, ins, outs):
    payloads, kept = outs[: len(counts)], list(outs[len(counts) :])
    filled = [0] * len(counts)
    ins = list(ins)
    for kind, count, payload, *rest in items:
        terms, ins = ins[:count], ins[count:]
        target, start = payloads[payload], filled[payload]
        if kind == "halve":
            bit, inner = rest
            mine = (here["dp"] >> bit) & 1
            out = kept.pop(0)
            for j in range(out.shape[0] // inner):
                for side, goal, base in ((1 - mine, target, start), (mine, out, 0)):
                    rows = pl.ds(pl.multiple_of((2 * j + side) * inner, 16), inner)
                    value = sum(term[rows, :].astype(F32) for term in terms)
                    goal[base + j * inner : base + (j + 1) * inner, :] = value.astype(BF)
            filled[payload] += out.shape[0]
        else:
            value = sum(term[...].astype(F32) for term in terms)
            target[start : start + value.shape[0], :] = value.astype(BF)
            filled[payload] += value.shape[0]
        if filled[payload] == counts[payload]:
            target.send()


def item_rows(item):
    kind, terms = item[:2]
    rows = terms[0].dims[0] if isinstance(terms[0], Arg) else terms[0].shape[0]
    return rows // 2 if kind == "halve" else rows


def stage(items, width):
    n_payloads = 1 + max(item[2] for item in items)
    counts, kept, places = [0] * n_payloads, [], []
    for item in items:
        rows = item_rows(item)
        places.append((item[2], counts[item[2]], rows))
        counts[item[2]] += rows
        if item[0] == "halve":
            kept.append(Held((rows, width), BF))
    outs = [shape((count, width), BF) for count in counts] + kept
    args = [term for item in items for term in item[1]]
    specs = [(item[0], len(item[1]), *item[2:]) for item in items]
    results = run(partial(stage_body, specs, counts), args, outs, 1000)
    return results[:n_payloads], list(results[n_payloads:]), places


def small_total(own, near, far, diagonal):
    shared = own[6:, :] + near[6:, :] + far[6:, :] + diagonal[6:, :]
    return own[0:1, :] + near[2:3, :], own[1:2, :] + near[3:4, :] + far[4:5, :] + diagonal[5:6, :], shared


def small_body(here, ins, outs):
    expand, heads, shared = small_total(*ins)
    outs[0][0:1, :] = expand
    outs[0][1:2, :] = heads
    outs[0][2 : 2 + shared.shape[0], :] = shared
    outs[0][2 + shared.shape[0] :, :] = jnp.zeros((SMALL - 2 - shared.shape[0], expand.shape[1]), F32)


def blocks_body(block, here, ins, outs):
    *terms, small, small_got = ins
    (out,) = outs
    low = (small[...] + small_got[...]).astype(BF)
    tall = block + SMALL
    for j in range(out.shape[0] // tall):
        rows = slice(j * block, (j + 1) * block)
        out[j * tall : j * tall + block, :] = sum(term[rows, :].astype(F32) for term in terms).astype(BF)
        out[j * tall + block : (j + 1) * tall, :] = low


def heads_body(part, here, ins, outs):
    (parts,) = ins
    g_query, g_key, g_value, g_output, small = outs
    block = g_query.shape[0]
    tall = block + SMALL
    count = parts.shape[0] // tall
    low = sum(parts[j * tall + block : (j + 1) * tall, :].astype(F32) for j in range(count))
    small[...] = low
    small.send()
    sums = sum(parts[j * tall : j * tall + block, :].astype(F32) for j in range(count))
    for i, out in enumerate((g_query, g_key, g_value)):
        out[...] = sums[:, i * part : (i + 1) * part]
        out.send()
    g_output[...] = sums[:, 3 * part :].T


def feeds_body(here, ins, outs):
    expand_a, expand_b, reduce_a, reduce_b = ins
    g_expand, g_reduce = outs
    g_expand[...] = expand_a[...].astype(F32) + expand_b[...].astype(F32)
    g_expand.send()
    g_reduce[...] = (reduce_a[...].astype(F32) + reduce_b[...].astype(F32)).T


def spread_body(*refs):
    ins, out, buffer, in_sems, out_sems = refs[:4], refs[4], refs[5], refs[6], refs[7]
    strip = lax.axis_index("mp")
    reads = [pltpu.make_async_copy(ins[s], buffer.at[s], in_sems.at[s]) for s in range(4)]
    writes = [pltpu.make_async_copy(buffer.at[s], out.at[strip ^ s], out_sems.at[s]) for s in range(4)]
    for read in reads:
        read.start()
    for read, write in zip(reads, writes):
        read.wait()
        write.start()
    for write in writes:
        write.wait()


def spread(strips):
    rows, width = strips[0].shape
    dtype = strips[0].dtype
    return pl.pallas_call(
        spread_body,
        in_specs=[ANY] * 4,
        out_specs=ANY,
        out_shape=shape((4, rows, width), dtype),
        scratch_shapes=[pltpu.VMEM((4, rows, width), dtype)] + [pltpu.SemaphoreType.DMA((4,))] * 2,
        cost_estimate=pl.CostEstimate(flops=0, bytes_accessed=16 * rows * width, transcendentals=0),
    )(*strips)


def swap(values, axis, size, bit):
    return lax.ppermute(values, axis, [(i, i ^ (1 << bit)) for i in range(size)])


def tie(*values):
    return lax.optimization_barrier(values)


def plain_sums(part, feeds, heads, small):
    def scattered(values):
        total = sum(v.astype(F32) for v in values)
        return lax.psum_scatter(total, "dp", scatter_dimension=0, tiled=True)

    g_expand, g_reduce = (scattered([v[i] for v in feeds]) for i in range(2))
    total = scattered(heads)
    g_query, g_key, g_value = (total[:, i * part : (i + 1) * part] for i in range(3))
    small = jnp.concatenate(small_total(*lax.psum((small, *others(small)), "dp")))
    return g_query, g_key, g_value, total[:, 3 * part :].T, g_expand, g_reduce.T, small


def others(small):
    return [lax.ppermute(small, "mp", [(i, i ^ k) for i in range(4)]) for k in (1, 2, 3)]


def total_of(*values):
    return sum(v.astype(F32) for v in values).astype(BF)


def arranged(result, grad_tokens, part, g_query, g_key, g_value, g_output, g_expand, g_reduce, small):
    b_reduce, b_output, gain_two, shift_two, gain_one, shift_one = (small[i] for i in range(2, 8))
    return (
        result,
        grad_tokens,
        g_query,
        small[1, :part],
        g_key,
        g_value,
        small[1, part : 2 * part],
        g_output,
        b_output,
        g_expand,
        small[0],
        g_reduce,
        b_reduce,
        gain_one,
        shift_one,
        gain_two,
        shift_two,
    )


def local(
    sizes,
    tokens,
    visible,
    w_query,
    b_query,
    w_key,
    w_value,
    b_value,
    w_output,
    b_output,
    w_expand,
    b_expand,
    w_reduce,
    b_reduce,
    gain_first,
    shift_first,
    gain_second,
    shift_second,
    cotangent,
):
    n_dp, n_mp = sizes
    part, units, (_, rows, width) = w_query.shape[1], w_expand.shape[1], tokens.shape
    core = partial(swap, axis="mp", size=n_mp, bit=0)
    across = partial(swap, axis="mp", size=n_mp, bit=1)
    over = [partial(swap, axis="dp", size=n_dp, bit=b) for b in range(n_dp.bit_length() - 1)]
    flat, tall, moved = Held((rows, width), BF), Held((width, rows), BF), shape((rows, width), BF)
    wide, rows8, rows16 = Held((rows, width), F32), Held((8, width), F32), shape((SMALL, width), F32)
    flop = 2 * rows * width * width
    block = width // n_dp
    halving = n_dp == 8 and block % 16 == 0

    third = 4 * part // 3
    direct, first, pack0, small0 = run(
        pack_body,
        (
            stacked(w_query.T, w_key.T, w_value.T, w_output, fixed=True),
            *(
                Arg([v], v.shape, fixed=True)
                for v in (
                    b_query,
                    b_value,
                    b_expand,
                    gain_first,
                    shift_first,
                    gain_second,
                    shift_second,
                    b_output,
                    b_reduce,
                )
            ),
        ),
        [
            shape((third, width), BF),
            shape((SMALL + third, width), BF),
            shape((4 * part, width), BF),
            shape((SMALL, width), BF),
        ],
        1000,
    )
    direct, first, pack1, small1 = across(direct), across(first), core(pack0), core(small0)
    n1, n1t = run(first_norm, (own(tokens), small0), (flat, tall), flop // 100)
    exp1, red1 = core(w_expand), core(w_reduce)
    n1, pack1, small1 = tie(n1, pack1, small1)
    near = run(near_attention, (held(n1), small0, pack0, small1, pack1), heads_shapes(rows, part, 2), 2 * flop, visible)
    *near, n1, direct, w_exp, w_red, cot, exp1, red1 = tie(
        *near, n1, direct, w_expand, w_reduce, cotangent, exp1, red1
    )
    relayed, direct3 = over[0](direct), core(direct)
    exp1, red1 = tie(exp1, red1)
    branch, branch_t, cross, cross_t, d_reduce, *d_hidden = run(
        branch_of,
        (own(cot), other(cot), held(w_red), held(red1)),
        (flat, tall, flat, tall, rows8, *[flat] * 4),
        flop // 100,
        visible,
    )
    branch, first, relayed = tie(branch, first, relayed)
    pack2, pack3 = (first, direct, relayed), (core(first), direct3, core(relayed))
    *pack3, branch, n1 = tie(*pack3, branch, n1)
    small2, small3 = rows_of(pack2[0], 0, SMALL), rows_of(pack3[0], 0, SMALL)
    pack2, pack3 = pieced(*pack2), pieced(*pack3)
    half, half_t = Held((rows // 2, width), BF), Held((width, rows // 2), BF)
    half_moved = shape((rows // 2, width), BF)
    *away, resid, n2, n2t, n2a, n2b = run(
        far_attention,
        (
            held(n1),
            small2,
            pack2,
            small3,
            pack3,
            held(near[5]),
            rows_of(pack0, 3 * part, part),
            rows_of(pack1, 3 * part, part),
            own(tokens),
            small0,
        ),
        [*heads_shapes(rows, part, 2), wide, flat, tall, half_moved, half_moved],
        3 * flop,
        visible,
    )
    n2a, n2b = across(n2a), across(n2b)
    grads = shape((2, width, units), BF)
    g0, g1, de_near, mlp, dn2 = run(
        near_feed,
        (
            *map(held, (n2, exp1, w_exp, red1, w_red, d_hidden[1], d_hidden[0], n2t, branch_t)),
            small1,
            small0,
        ),
        [grads, grads, rows8, wide, wide],
        12 * flop,
    )

    def cross_half(normed, first):
        gradients = [held(v, first, rows // 2) for v in (d_hidden[3], d_hidden[2])]
        return run(
            cross_feed,
            (normed, held(exp1), held(w_exp), *gradients, small1, small0),
            [half, half, half, half, half_t, half_moved],
            3 * flop,
        )

    g0, g1, n2a = tie(g0, g1, n2a)
    *half_a, dn2_back = cross_half(n2a, 0)
    got_a = across(dn2_back)
    half_a[0], n2b = tie(half_a[0], n2b)
    *half_b, dn2_back = cross_half(n2b, rows // 2)
    got_b = across(dn2_back)
    near_a, near_b = ([held(v) for v in (h[0], h[1], h[4])] for h in (half_a, half_b))
    g1, de_one = run(
        cross_one, (held(cross_t), g1, held(de_near), *near_a, *near_b), [grads, rows8], 2 * flop
    )
    g1, de_one, got_a = tie(g1, de_one, got_a)
    got0 = core(g1)
    near_a, near_b = ([held(v) for v in (h[0], h[2], h[3], h[4])] for h in (half_a, half_b))
    de_near, g1 = tie(de_near, g1)
    g0, de_zero, mlp_back = run(
        cross_zero,
        (held(cross_t), g0, *map(held, (de_near, red1, w_red)), *near_a, *near_b),
        [grads, rows8, moved],
        4 * flop,
    )
    if halving:
        g0, got0, mlp_back = tie(g0, got0, mlp_back)
    mlp_got = across(mlp_back)
    if halving:
        (pay_x, pay_z), (kept_e, kept_r), _ = stage(
            [
                ("halve", (entry(g0, 0), entry(got0, 0)), 0, 0, block),
                ("halve", (entry(g0, 1), entry(got0, 1)), 1, 1, 2 * block),
            ],
            width,
        )
        got_e, got_r = over[0](pay_x), over[1](pay_z)
        got_b, kept_e = tie(got_b, kept_e)
    grads = shape((width, 4 * part), BF)
    extra = (pltpu.VMEM((rows, 3 * part), BF), pltpu.VMEM((1, width), F32))

    def saved_of(saved, s):
        n = part // HD
        return [held(a, s * n, n) for a in saved[:5]] + [held(saved[5])]

    h2, h3, ds_far, dn1, grad_resid, attn, attn_t, sums2 = run(
        far_back,
        (
            held(resid),
            held(dn2),
            stacked(got_a, got_b),
            held(branch),
            small0,
            pack3,
            held(n1t),
            *map(held, away),
            pack2,
        ),
        [grads, grads, rows8, wide, wide, flat, tall, rows8],
        8 * flop,
        scratch=extra,
    )
    if halving:
        h2, h3, attn, mlp_got, got_e, got_r, kept_e = tie(h2, h3, attn, mlp_got, got_e, got_r, kept_e)
    got_h2 = core(h3)

    def back(column, attn, pack, saved, d_norm):
        return run(
            partial(slot_back, column),
            (held(attn), pack, held(attn_t), held(n1t), *saved_of(saved, column), held(d_norm)),
            [*[shape((width // 2, 4 * part), BF)] * 2, rows8, wide],
            4 * flop,
            scratch=extra,
        )

    h2, mlp_got = tie(h2, mlp_got)
    (result,) = run(
        result_body, (held(resid), held(mlp), mlp_got, small0), [shape((rows, width), BF)], flop // 100, visible
    )
    if halving:
        result_far, result_near = across(result), core(result)
        result, h2, got_h2, attn = tie(result, h2, got_h2, attn)
        (pay_z, pay_x, pay_h), (kept_e, kept_r, kept_h), _ = stage(
            [
                ("halve", (held(kept_e), got_e), 0, 1, block),
                ("halve", (held(kept_r), got_r), 1, 0, block),
                ("halve", (h2, got_h2), 2, 0, block),
            ],
            width,
        )
        got_z, got_x, got_h = over[1](pay_z), over[0](pay_x), over[0](pay_h)
        attn, kept_e, result_near = tie(attn, kept_e, result_near)
    *h1, ds1, dn1 = back(1, attn, pack1, near, dn1)
    if halving:
        attn, got_z, got_x, kept_e, *h1 = tie(attn, got_z, got_x, kept_e, *h1)
    got_h0 = [core(v) for v in h1]
    if halving:
        (pay_w,), (kept_e, kept_r), places_w = stage(
            [("halve", (held(kept_e), got_z), 0, 2, block), ("halve", (held(kept_r), got_x), 0, 2, block)], width
        )
        got_w = over[2](pay_w)
        attn, kept_e = tie(attn, kept_e)
    h0, strip, small = run(
        last_back,
        (
            held(attn),
            pack0,
            held(attn_t),
            held(n1t),
            *saved_of(near, 0),
            held(dn1),
            own(tokens),
            held(grad_resid),
            small0,
            *map(held, (de_zero, de_one, ds_far, ds1, d_reduce, sums2)),
        ),
        [grads, shape((rows, width), BF), rows16],
        4 * flop,
        scratch=extra,
    )
    if not halving:
        grad_tokens, result = (spread([v, core(v), across(v), core(across(v))]) for v in (strip, result))
        heads_got = across(total_of(h2, got_h2))
        sums = plain_sums(part, (g0, got0), (h0, jnp.concatenate(got_h0), heads_got), small)
        return arranged(result, grad_tokens, part, *sums)
    h0, strip, small, got_h, result_far, *got_h0 = tie(h0, strip, small, got_h, result_far, *got_h0)
    (pay_y, pay_x), (kept_h0,), _ = stage(
        [("sum", (held(kept_h), got_h), 0), ("halve", (h0, stacked(*got_h0)), 1, 0, block)], width
    )
    got_h0, heads_got = over[0](pay_x), across(pay_y)
    kept_h0, small = tie(kept_h0, small)
    small_got = others(small)
    kept_h0, strip, got_w, *small_got = tie(kept_h0, strip, got_w, *small_got)
    (small,) = run(small_body, (small, *small_got), [rows16], 1000)
    small_got = over[0](small)
    strip_far, strip_near, result_diag = across(strip), core(strip), core(result_far)
    small, kept_h0, result, result_diag = tie(small, kept_h0, result, result_diag)
    first_w, second_w = (rows_of(got_w, place[1], place[2]) for place in places_w)
    g_expand, g_reduce = run(
        feeds_body,
        (held(kept_e), first_w, held(kept_r), second_w),
        [shape((block, units), F32), shape((units, block), F32)],
        1000,
    )
    result = spread([result, result_near, result_far, result_diag])
    result, g_expand, kept_h0, got_h0, heads_got, small_got = tie(
        result, g_expand, kept_h0, got_h0, heads_got, small_got
    )
    column = n_dp // 2
    (sums,) = run(
        partial(blocks_body, block),
        (held(kept_h0), got_h0, heads_got, small, small_got),
        [shape((column * (block + SMALL), width), BF)],
        1000,
    )
    columns = [[2 * z + x for z in range(column)] for x in range(2)]
    sums_got = lax.all_to_all(sums, "dp", 0, 0, axis_index_groups=columns, tiled=True)
    sums, strip_far = tie(sums, strip_far)
    strip_diag = core(strip_far)
    sums, strip_diag = tie(sums, strip_diag)
    grad_tokens = spread([strip, strip_near, strip_far, strip_diag])
    grad_tokens, sums_got = tie(grad_tokens, sums_got)
    narrow, thin = shape((block, part), F32), shape((part, block), F32)
    *heads, small = run(partial(heads_body, part), (sums_got,), [narrow, narrow, narrow, thin, rows16], 1000)
    return arranged(result, grad_tokens, part, *heads, g_expand, g_reduce, small)


def solution(mesh):
    placed = (
        P("dp", None, None),
        P("dp"),
        P(None, "mp"),
        P("mp"),
        P(None, "mp"),
        P(None, "mp"),
        P("mp"),
        P("mp", None),
        P(),
        P(None, "mp"),
        P("mp"),
        P("mp", None),
        P(),
        P(),
        P(),
        P(),
        P(),
        P("dp", None, None),
    )
    return jax.shard_map(
        partial(local, (mesh.shape["dp"], mesh.shape["mp"])),
        mesh=mesh,
        in_specs=placed,
        out_specs=(
            P("dp", None, None),
            P("dp", None, None),
            P("dp", "mp"),
            P("mp"),
            P("dp", "mp"),
            P("dp", "mp"),
            P("mp"),
            P("mp", "dp"),
            P(),
            P("dp", "mp"),
            P("mp"),
            P("mp", "dp"),
            P(),
            P(),
            P(),
            P(),
            P(),
        ),
        check_vma=False,
    )
```

```python
from functools import partial

import jax
import jax.numpy as jnp
from jax import lax
from jax.experimental import pallas as pl
from jax.experimental.pallas import tpu as pltpu
from jax.sharding import PartitionSpec as P

HD = 64
F32 = jnp.float32
BF = jnp.bfloat16
NT = (((1,), (1,)), ((), ()))
ANY = pl.BlockSpec(memory_space=pl.ANY)
SMEM = pl.BlockSpec(memory_space=pltpu.SMEM)
VMEM = pl.BlockSpec(memory_space=pltpu.VMEM)


def dot(left, right):
    return jnp.dot(left, right, preferred_element_type=F32)


def dot_nt(left, right):
    return lax.dot_general(left, right, NT, preferred_element_type=F32)


def shape(dims, dtype):
    return jax.ShapeDtypeStruct(dims, dtype)


class Load:
    def __init__(self, buffer, copies=()):
        self.buffer, self.copies = buffer, copies
        for copy in copies:
            copy.start()

    def ref(self):
        for copy in self.copies:
            copy.wait()
        self.copies = ()
        return self.buffer

    def __getitem__(self, index):
        return self.ref()[index]

    @property
    def shape(self):
        return self.buffer.shape


class Store:
    def __init__(self, buffer, target=None, sems=None):
        self.target, self.buffer, self.sems = target, buffer, sems
        self.copies = []

    def start(self, source, target):
        self.copies.append(pltpu.make_async_copy(source, target, self.sems.at[len(self.copies)]))
        self.copies[-1].start()

    def send(self, *index):
        if self.target is not None:
            self.start(*((self.buffer.at[index], self.target.at[index]) if index else (self.buffer, self.target)))

    def send_from(self, view):
        self.start(view, self.target)

    def close(self):
        if not self.copies:
            self.send()
        for copy in self.copies:
            copy.wait()

    def __setitem__(self, index, value):
        self.buffer[index] = value

    def __getitem__(self, index):
        return self.buffer[index]

    @property
    def shape(self):
        return self.buffer.shape


class Held:
    def __init__(self, dims, dtype):
        self.struct = shape(dims, dtype)


PIECES = 8
SMALL = 16


class Arg:
    def __init__(self, arrays, dims, view=None, offset=None, counts=None, held=False, firsts=None, fixed=False):
        self.arrays, self.dims, self.view, self.offset, self.held = arrays, dims, view, offset, held
        self.fixed = fixed
        self.firsts = firsts or [0] * len(arrays)
        self.counts = counts or [a.shape[0] for a in arrays]


def own(array):
    return Arg([array], array.shape[1:], view=lambda ref, here: ref.at[here["strip"]], fixed=True)


def other(array):
    return Arg([array], array.shape[1:], view=lambda ref, here: ref.at[here["strip"] ^ 2], fixed=True)


def entry(array, index):
    return Arg([array], array.shape[1:], view=lambda ref, here: ref.at[index])


def held(array, first=None, count=None):
    if first is None:
        return Arg([array], array.shape, held=True)
    view = lambda ref, here: ref.at[pl.ds(first, count)]
    return Arg([array], (count, *array.shape[1:]), view=view, held=True)


def rows_of(array, first, count):
    return Arg([array], (count, *array.shape[1:]), view=lambda ref, here: ref.at[pl.ds(first, count)])


def stacked(*arrays, counts=None, fixed=False):
    counts = counts or [a.shape[0] for a in arrays]
    starts = [sum(counts[:i]) for i in range(len(counts))]
    dims = (sum(counts), arrays[0].shape[1])
    return Arg(list(arrays), dims, offset=lambda here: starts, counts=counts, fixed=fixed)


def pieced(first, direct, relayed):
    base, count = first.shape[0], direct.shape[0]

    def offset(here):
        bit = here["bit"]
        return (
            0,
            pl.multiple_of(base + count * bit, 16),
            pl.multiple_of(base + count * (1 - bit), 16),
        )

    return Arg([first, direct, relayed], (base + 2 * count, first.shape[1]), offset=offset)


LIMIT = 17


def run(body, args, outs, flops, visible=None, scratch=()):
    args = [a if isinstance(a, Arg) else Arg([a], a.shape) for a in args]
    arrays = [array for a in args for array in a.arrays]
    loaded = [a for a in args if not a.held]
    stay = [isinstance(o, Held) for o in outs]
    structs = [o.struct if isinstance(o, Held) else o for o in outs]
    n_arrays, n_out, n_stored = len(arrays), len(outs), len(outs) - sum(stay)

    def kernel(*refs):
        here = {"strip": lax.axis_index("mp"), "bit": lax.axis_index("dp") & 1, "dp": lax.axis_index("dp")}
        if visible is not None:
            visible_ref, *refs = refs
            here["visible"] = visible_ref[here["strip"]]
            here["visible_across"] = visible_ref[here["strip"] ^ 2]
        ins, results, refs = refs[:n_arrays], refs[n_arrays : n_arrays + n_out], refs[n_arrays + n_out :]
        in_buffers, refs = list(refs[: len(loaded)]), refs[len(loaded) :]
        out_buffers, (in_sems, out_sems, *rest) = list(refs[:n_stored]), refs[n_stored:]
        loads, j = [], 0
        for a in args:
            if a.held:
                loads.append(Load(ins[j] if a.view is None else a.view(ins[j], here)))
                j += 1
                continue
            buffer, copies = in_buffers.pop(0), []
            offsets = a.offset(here) if a.offset is not None else None
            for i, array in enumerate(a.arrays):
                source = a.view(ins[j], here) if a.view is not None else ins[j]
                target = buffer if offsets is None else buffer.at[pl.ds(offsets[i], a.counts[i])]
                if offsets is not None and a.counts[i] < array.shape[0]:
                    source = source.at[pl.ds(a.firsts[i], a.counts[i])]
                copies.append(pltpu.make_async_copy(source, target, in_sems.at[j]))
                j += 1
            loads.append(Load(buffer, copies))
        stores = []
        for i, (result, stays) in enumerate(zip(results, stay)):
            stores.append(Store(result) if stays else Store(out_buffers.pop(0), result, out_sems.at[i]))
        body(here, loads, stores, *rest)
        for load in loads:
            load.ref()
        for store in stores:
            store.close()

    moved = sum(a.size * a.dtype.itemsize for a in [*arrays, *structs])
    scratches = [pltpu.VMEM(a.dims, a.arrays[0].dtype) for a in loaded]
    scratches += [pltpu.VMEM(o.shape, o.dtype) for o, stays in zip(structs, stay) if not stays]
    scratches += [pltpu.SemaphoreType.DMA((n_arrays,)), pltpu.SemaphoreType.DMA((n_out, PIECES))]
    return pl.pallas_call(
        kernel,
        in_specs=[SMEM] * (visible is not None) + [VMEM if a.held else ANY for a in args for _ in a.arrays],
        out_specs=tuple(VMEM if stays else ANY for stays in stay),
        out_shape=tuple(structs),
        scratch_shapes=scratches + list(scratch),
        cost_estimate=pl.CostEstimate(flops=flops, bytes_accessed=moved, transcendentals=0),
        compiler_params=pltpu.CompilerParams(vmem_limit_bytes=LIMIT << 20),
    )(
        *([] if visible is None else [visible]),
        *(
            pltpu.with_memory_space_constraint(array, pltpu.HBM) if a.fixed else array
            for a in args
            for array in a.arrays
        ),
    )


def norm_parts(values):
    center = values - jnp.mean(values, axis=-1, keepdims=True)
    rstd = lax.rsqrt(jnp.mean(center * center, axis=-1, keepdims=True) + 1e-06)
    return center * rstd, rstd


def norm_back(unit, rstd, gain, grad):
    scaled = grad * gain
    first = jnp.mean(scaled, axis=-1, keepdims=True)
    second = jnp.mean(scaled * unit, axis=-1, keepdims=True)
    return rstd * (scaled - first - unit * second)


def row_sum(values):
    return jnp.sum(values, axis=0, keepdims=True)


BIAS_EXPAND, BIAS_HEADS, GAIN_ONE, SHIFT_ONE, GAIN_TWO, SHIFT_TWO, BIAS_OUT, BIAS_REDUCE = range(8)


def vector(vectors, row):
    return vectors[row : row + 1, :].astype(F32)


def pack_body(here, ins, outs):
    pieces, b_query, b_value, *vectors = ins
    choice, first, pack, small = outs
    rows = pieces.ref()
    third = choice.shape[0]
    choice.send_from(rows.at[pl.ds(pl.multiple_of(third * (1 + here["bit"]), 16), third)])
    first.start(rows.at[pl.ds(0, third)], first.target.at[pl.ds(SMALL, third)])
    pack.send_from(rows)
    small[...] = jnp.zeros(small.shape, BF)
    part = b_query.shape[0]
    small[BIAS_HEADS : BIAS_HEADS + 1, :part] = b_query[...].reshape(1, part)
    small[BIAS_HEADS : BIAS_HEADS + 1, part : 2 * part] = b_value[...].reshape(1, part)
    rows_of_vectors = (BIAS_EXPAND, GAIN_ONE, SHIFT_ONE, GAIN_TWO, SHIFT_TWO, BIAS_OUT, BIAS_REDUCE)
    for row, values in zip(rows_of_vectors, vectors):
        small[row : row + 1, :] = values[...].reshape(1, values.shape[0])
    first.start(small.buffer, first.target.at[pl.ds(0, SMALL)])
    small.send()


def first_norm(here, ins, outs):
    tok, vectors = ins
    normed, normed_t = outs
    unit, _ = norm_parts(tok[...].astype(F32))
    low = (unit * vector(vectors, GAIN_ONE) + vector(vectors, SHIFT_ONE)).astype(BF)
    normed[...] = low
    normed_t[...] = low.T


def branch_of(here, ins, outs):
    cot, cross, red0, red1 = ins
    total, hidden = outs[4], outs[5:]
    for i, (strip, name) in enumerate(((cot, "visible"), (cross, "visible_across"))):
        branch, branch_t = outs[2 * i : 2 * i + 2]
        row = lax.broadcasted_iota(jnp.int32, strip.shape, 0)
        kept = jnp.where(row < here[name], strip[...].astype(F32), 0.0)
        low = kept.astype(BF)
        branch[...] = low
        branch_t[...] = low.T
        hidden[2 * i][...] = dot_nt(low, red0[...]).astype(BF)
        hidden[2 * i + 1][...] = dot_nt(low, red1[...]).astype(BF)
        if i == 0:
            total[...] = jnp.broadcast_to(row_sum(kept), total.shape)


def heads_forward(here, normed, smalls, packs, outs):
    q_out, k_out, v_out, e_out, o_out, ctx_out = outs
    rows, width = normed.shape
    part = width // 4
    heads = part // HD
    lane = lax.broadcasted_iota(jnp.int32, (rows, HD), 1)
    row = lax.broadcasted_iota(jnp.int32, (rows, HD), 0)
    one = jnp.where(lane == 0, 1.0, 0.0).astype(BF)
    mask = jnp.where((lane == 0) & (row >= here["visible"]), -1e30, 0.0).astype(BF)
    low = normed[...]
    for s, pack in enumerate(packs):
        biases = vector(smalls[s], BIAS_HEADS)
        at = pack.shape[0] - 4 * part
        rows_q, rows_k, rows_v = (slice(at + i * part, at + (i + 1) * part) for i in range(3))
        q = (dot_nt(low, pack[rows_q, :]) + biases[:, :part]).astype(BF) * BF(HD**-0.5)
        k = dot_nt(low, pack[rows_k, :]).astype(BF)
        v = (dot_nt(low, pack[rows_v, :]) + biases[:, part : 2 * part]).astype(BF)
        for h in range(heads):
            cols = slice(h * HD, (h + 1) * HD)
            i = s * heads + h
            q_out[i, :, :HD] = q[:, cols]
            q_out[i, :, HD:] = one
            k_out[i, :, :HD] = k[:, cols]
            k_out[i, :, HD:] = mask
            v_out[i, :, :HD] = v[:, cols]
            v_out[i, :, HD:] = one
    for out in (q_out, k_out, v_out):
        out.send()
    for i in range(len(packs) * heads):
        scores = dot_nt(q_out[i], k_out[i])
        e = jnp.exp(scores - jnp.max(scores, axis=1, keepdims=True)).astype(BF)
        e_out[i] = e
        e_out.send(i)
        o = dot(e, v_out[i])
        o_out[i] = o
        ctx_out[:, i * HD : (i + 1) * HD] = (o[:, :HD] * (1.0 / o[:, HD : HD + 1])).astype(BF)
    o_out.send()
    ctx_out.send()


def heads_shapes(rows, part, slots):
    n = slots * part // HD
    outs = [Held((n, rows, 2 * HD), BF)] * 3
    return outs + [Held((n, rows, rows), BF), Held((n, rows, 2 * HD), F32), Held((rows, n * HD), BF)]


def near_attention(here, ins, outs):
    normed, small0, pack0, small1, pack1 = ins
    heads_forward(here, normed, (small0, small1), (pack0, pack1), outs)


def far_attention(here, ins, outs):
    normed, small2, pack2, small3, pack3, ctx, wo0, wo1, tok, vectors = ins
    heads_forward(here, normed, (small2, small3), (pack2, pack3), outs[:6])
    resid, normed_two, normed_two_t, *halves = outs[6:]
    part = wo0.shape[0]
    total = tok[...].astype(F32) + vector(vectors, BIAS_OUT)
    total += dot(ctx[:, :part], wo0[...]) + dot(ctx[:, part:], wo1[...])
    far = outs[5]
    total += dot(far[:, :part], pack2[-part:, :])
    total += dot(far[:, part:], pack3[-part:, :])
    resid[...] = total
    resid.send()
    unit, _ = norm_parts(total)
    low = (unit * vector(vectors, GAIN_TWO) + vector(vectors, SHIFT_TWO)).astype(BF)
    normed_two[...] = low
    count = halves[0].shape[0]
    for i, half in enumerate(halves):
        half.send_from(normed_two.buffer.at[pl.ds(i * count, count)])
    normed_two_t[...] = low.T


def hidden_of(normed, d_hidden, small, we):
    pre = dot(normed[...], we[...]) + vector(small, BIAS_EXPAND)
    cdf = 0.5 * (1.0 + lax.erf(pre * 0.7071067811865476))
    slope = cdf + pre * (jnp.exp(-0.5 * pre * pre) * 0.3989422804014327)
    return (pre * cdf).astype(BF), (d_hidden[...].astype(F32) * slope).astype(BF)


def near_feed(here, ins, outs):
    normed, exp1, exp0, red1, red0, d_hidden1, d_hidden0, normed_t, branch_t, small1, small0 = ins
    grad0, grad1, d_small, mlp, d_norm = outs
    total, back = None, None
    for s, (grads, we, wr, d_hidden, small) in enumerate(
        ((grad1, exp1, red1, d_hidden1, small1), (grad0, exp0, red0, d_hidden0, small0))
    ):
        hidden, d_pre = hidden_of(normed, d_hidden, small, we)
        grads[0] = dot(normed_t[...], d_pre).astype(BF)
        grads.send(0)
        grads[1] = dot(branch_t[...], hidden).astype(BF)
        grads.send(1)
        d_small[s : s + 1, :] = row_sum(d_pre.astype(F32))
        out = dot(hidden, wr[...])
        total = out if total is None else total + out
        out = dot_nt(d_pre, we[...])
        back = out if back is None else back + out
    mlp[...], d_norm[...] = total, back


def cross_feed(here, ins, outs):
    normed, exp1, exp0, d_hidden1, d_hidden0, small1, small0 = ins
    hidden1, d_pre1, hidden0, d_pre0, normed_t, d_norm = outs
    h, d = hidden_of(normed, d_hidden1, small1, exp1)
    hidden1[...], d_pre1[...] = h, d
    back = dot_nt(d, exp1[...])
    h, d = hidden_of(normed, d_hidden0, small0, exp0)
    hidden0[...], d_pre0[...] = h, d
    normed_t[...] = normed[...].T
    d_norm[...] = (back + dot_nt(d, exp0[...])).astype(BF)


def cross_slot(grads, d_small, cross_t, part, d_near, halves, hidden, d_pre):
    rows = halves[0][0].shape[0]

    def over_halves(left, right):
        return sum(dot(left(i), right(i)) for i in range(2))

    grads[1] = (
        over_halves(lambda i: cross_t[:, i * rows : (i + 1) * rows], lambda i: halves[i][hidden][...])
        + part[1].astype(F32)
    ).astype(BF)
    grads.send(1)
    grads[0] = (
        over_halves(lambda i: halves[i][-1][...], lambda i: halves[i][d_pre][...]) + part[0].astype(F32)
    ).astype(BF)
    grads.send(0)
    d_small[0:1, :] = d_near + sum(row_sum(halves[i][d_pre][...].astype(F32)) for i in range(2))


def cross_one(here, ins, outs):
    cross_t, part, d_near, *halves = ins
    count = len(halves) // 2
    cross_slot(outs[0], outs[1], cross_t, part, d_near[0:1, :], (halves[:count], halves[count:]), 0, 1)


def cross_zero(here, ins, outs):
    cross_t, part, d_near, red1, red0, *halves = ins
    grads, d_small, mlp = outs
    count = len(halves) // 2
    halves = halves[:count], halves[count:]
    rows = halves[0][0].shape[0]
    cross_slot(grads, d_small, cross_t, part, d_near[1:2, :], halves, 1, 2)
    for i in range(2):
        out = dot(halves[i][0][...], red1[...]) + dot(halves[i][1][...], red0[...])
        mlp[i * rows : (i + 1) * rows, :] = out.astype(BF)


def heads_backward(attn, attn_t, normed_t, saved, s, column, pack, grads, d_small, d_in):
    q_in, k_in, v_in, e_in, o_in, ctx = saved
    part = ctx.shape[1] // 2
    at_pack = pack.shape[0] - 4 * part
    heads = part // HD
    d_ctx = dot_nt(attn[...], pack[at_pack + 3 * part :, :]).astype(BF).astype(F32)
    back_v, back_k = [], []
    for h in range(s * heads, (s + 1) * heads):
        o = o_in[h]
        inverse = 1.0 / o[:, HD : HD + 1]
        at = h - s * heads
        do = (d_ctx[:, at * HD : (at + 1) * HD] * inverse).astype(BF)
        term = jnp.sum(do.astype(F32) * o[:, :HD], axis=1, keepdims=True) * inverse
        e = e_in[h]
        d_prob = dot_nt(do, v_in[h][:, :HD])
        d_score = (e.astype(F32) * (d_prob - term)).astype(BF)
        back_v.append(dot(do.T, e))
        back_k.append(dot(q_in[h][:, :HD].T, d_score))
        d_in[:, at * HD : (at + 1) * HD] = (dot(d_score, k_in[h][:, :HD]) * HD**-0.5).astype(BF)
    d_in[:, part : 2 * part] = jnp.concatenate(back_k, axis=0).T.astype(BF)
    d_in[:, 2 * part :] = jnp.concatenate(back_v, axis=0).T.astype(BF)
    grads[:, : 3 * part] = dot(normed_t[...], d_in[...]).astype(BF)
    grads[:, 3 * part :] = dot(attn_t[...], ctx[:, column * part : (column + 1) * part]).astype(BF)
    grads.send()
    d_small[:, :part] = row_sum(d_in[:, :part].astype(F32))
    d_small[:, part : 2 * part] = row_sum(d_in[:, 2 * part :].astype(F32))
    return dot(d_in[...], pack[at_pack : at_pack + 3 * part, :])


def far_back(here, ins, outs, d_in, d_row):
    resid, d_norm, got, branch, vectors, pack3, normed_t, *saved, pack2 = ins
    grad2, grad3, d_small, out, grad, attn, attn_t, sums = outs
    unit, rstd = norm_parts(resid[...])
    dn = d_norm[...] + got[...].astype(F32)
    g = branch[...].astype(F32) + norm_back(unit, rstd, vector(vectors, GAIN_TWO), dn)
    grad[...] = g
    grad.send()
    low = g.astype(BF)
    attn[...] = low
    attn.send()
    attn_t[...] = low.T
    attn_t.send()
    sums[0:1, :] = row_sum(low.astype(F32))
    sums[1:2, :] = row_sum(dn * unit)
    sums[2:3, :] = row_sum(dn)
    d_row[...] = jnp.zeros(d_row.shape, F32)
    back = heads_backward(attn, attn_t, normed_t, saved, 1, 1, pack3, grad3, d_row, d_in)
    d_small[0:1, :] = d_row[...]
    back = back + heads_backward(attn, attn_t, normed_t, saved, 0, 0, pack2, grad2, d_row, d_in)
    d_small[1:2, :] = d_row[...]
    out[...] = back


def result_body(here, ins, outs):
    resid, mlp, got, vectors = ins
    row = lax.broadcasted_iota(jnp.int32, resid.shape, 0)
    total = resid[...] + (mlp[...] + got[...].astype(F32) + vector(vectors, BIAS_REDUCE))
    outs[0][...] = jnp.where(row < here["visible"], total, 0.0).astype(BF)


class Rows:
    def __init__(self, parts):
        self.parts = parts

    def __setitem__(self, index, value):
        rows, columns = index
        start = 0
        for part in self.parts:
            count = part.shape[0]
            part[:, columns] = value[start : start + count, :]
            start += count

    def send(self):
        for part in self.parts:
            part.send()


def slot_back(column, here, ins, outs, d_in, d_row):
    attn, pack, attn_t, normed_t, *saved, d_norm = ins
    grads, (d_small, out) = Rows(outs[:-2]), outs[-2:]
    d_row[...] = jnp.zeros(d_row.shape, F32)
    dn = heads_backward(attn, attn_t, normed_t, saved, 0, column, pack, grads, d_row, d_in)
    d_small[0:1, :] = d_row[...]
    out[...] = d_norm[...] + dn


def last_back(here, ins, outs, d_in, d_row):
    attn, pack, attn_t, normed_t, *rest = ins
    saved, (d_norm, tok, grad, vectors, *small) = rest[:6], rest[6:]
    grads, out, small_out = outs
    d_row[...] = jnp.zeros(d_row.shape, F32)
    dn = d_norm[...] + heads_backward(
        attn, attn_t, normed_t, saved, 0, 0, pack, grads, d_row, d_in
    )
    unit, rstd = norm_parts(tok[...].astype(F32))
    out[...] = (grad[...] + norm_back(unit, rstd, vector(vectors, GAIN_ONE), dn)).astype(BF)
    out.send()
    feed0, feed1, d_far, d_one, d_reduce, sums = small
    small_out[...] = jnp.zeros(small_out.shape, F32)
    late = [feed0[0:1, :], d_row[...], feed1[0:1, :], d_one[0:1, :], d_far[1:2, :], d_far[0:1, :]]
    late += [d_reduce[0:1, :], sums[0:3, :], row_sum(dn * unit), row_sum(dn)]
    start = 0
    for values in late:
        small_out[start : start + values.shape[0], :] = values
        start += values.shape[0]


def stage_body(items, counts, here, ins, outs):
    payloads, kept = outs[: len(counts)], list(outs[len(counts) :])
    filled = [0] * len(counts)
    ins = list(ins)
    for kind, count, payload, *rest in items:
        terms, ins = ins[:count], ins[count:]
        target, start = payloads[payload], filled[payload]
        if kind == "halve":
            bit, inner = rest
            mine = (here["dp"] >> bit) & 1
            out = kept.pop(0)
            for j in range(out.shape[0] // inner):
                for side, goal, base in ((1 - mine, target, start), (mine, out, 0)):
                    rows = pl.ds(pl.multiple_of((2 * j + side) * inner, 16), inner)
                    value = sum(term[rows, :].astype(F32) for term in terms)
                    goal[base + j * inner : base + (j + 1) * inner, :] = value.astype(BF)
            filled[payload] += out.shape[0]
        else:
            value = sum(term[...].astype(F32) for term in terms)
            target[start : start + value.shape[0], :] = value.astype(BF)
            filled[payload] += value.shape[0]
        if filled[payload] == counts[payload]:
            target.send()


def item_rows(item):
    kind, terms = item[:2]
    rows = terms[0].dims[0] if isinstance(terms[0], Arg) else terms[0].shape[0]
    return rows // 2 if kind == "halve" else rows


def stage(items, width):
    n_payloads = 1 + max(item[2] for item in items)
    counts, kept, places = [0] * n_payloads, [], []
    for item in items:
        rows = item_rows(item)
        places.append((item[2], counts[item[2]], rows))
        counts[item[2]] += rows
        if item[0] == "halve":
            kept.append(Held((rows, width), BF))
    outs = [shape((count, width), BF) for count in counts] + kept
    args = [term for item in items for term in item[1]]
    specs = [(item[0], len(item[1]), *item[2:]) for item in items]
    results = run(partial(stage_body, specs, counts), args, outs, 1000)
    return results[:n_payloads], list(results[n_payloads:]), places


def small_total(own, near, far, diagonal):
    shared = own[6:, :] + near[6:, :] + far[6:, :] + diagonal[6:, :]
    return own[0:1, :] + near[2:3, :], own[1:2, :] + near[3:4, :] + far[4:5, :] + diagonal[5:6, :], shared


def small_body(here, ins, outs):
    expand, heads, shared = small_total(*ins)
    outs[0][0:1, :] = expand
    outs[0][1:2, :] = heads
    outs[0][2 : 2 + shared.shape[0], :] = shared
    outs[0][2 + shared.shape[0] :, :] = jnp.zeros((SMALL - 2 - shared.shape[0], expand.shape[1]), F32)


def blocks_body(block, here, ins, outs):
    *terms, small, small_got = ins
    (out,) = outs
    low = (small[...] + small_got[...]).astype(BF)
    tall = block + SMALL
    for j in range(out.shape[0] // tall):
        rows = slice(j * block, (j + 1) * block)
        out[j * tall : j * tall + block, :] = sum(term[rows, :].astype(F32) for term in terms).astype(BF)
        out[j * tall + block : (j + 1) * tall, :] = low


def heads_body(part, here, ins, outs):
    (parts,) = ins
    g_query, g_key, g_value, g_output, small = outs
    block = g_query.shape[0]
    tall = block + SMALL
    count = parts.shape[0] // tall
    low = sum(parts[j * tall + block : (j + 1) * tall, :].astype(F32) for j in range(count))
    small[...] = low
    small.send()
    sums = sum(parts[j * tall : j * tall + block, :].astype(F32) for j in range(count))
    for i, out in enumerate((g_query, g_key, g_value)):
        out[...] = sums[:, i * part : (i + 1) * part]
        out.send()
    g_output[...] = sums[:, 3 * part :].T


def feeds_body(here, ins, outs):
    expand_a, expand_b, reduce_a, reduce_b = ins
    g_expand, g_reduce = outs
    g_expand[...] = expand_a[...].astype(F32) + expand_b[...].astype(F32)
    g_expand.send()
    g_reduce[...] = (reduce_a[...].astype(F32) + reduce_b[...].astype(F32)).T


def spread_body(*refs):
    ins, out, buffer, in_sems, out_sems = refs[:4], refs[4], refs[5], refs[6], refs[7]
    strip = lax.axis_index("mp")
    reads = [pltpu.make_async_copy(ins[s], buffer.at[s], in_sems.at[s]) for s in range(4)]
    writes = [pltpu.make_async_copy(buffer.at[s], out.at[strip ^ s], out_sems.at[s]) for s in range(4)]
    for read in reads:
        read.start()
    for read, write in zip(reads, writes):
        read.wait()
        write.start()
    for write in writes:
        write.wait()


def spread(strips):
    rows, width = strips[0].shape
    dtype = strips[0].dtype
    return pl.pallas_call(
        spread_body,
        in_specs=[ANY] * 4,
        out_specs=ANY,
        out_shape=shape((4, rows, width), dtype),
        scratch_shapes=[pltpu.VMEM((4, rows, width), dtype)] + [pltpu.SemaphoreType.DMA((4,))] * 2,
        cost_estimate=pl.CostEstimate(flops=0, bytes_accessed=16 * rows * width, transcendentals=0),
    )(*strips)


def swap(values, axis, size, bit):
    return lax.ppermute(values, axis, [(i, i ^ (1 << bit)) for i in range(size)])


def tie(*values):
    return lax.optimization_barrier(values)


def plain_sums(part, feeds, heads, small):
    def scattered(values):
        total = sum(v.astype(F32) for v in values)
        return lax.psum_scatter(total, "dp", scatter_dimension=0, tiled=True)

    g_expand, g_reduce = (scattered([v[i] for v in feeds]) for i in range(2))
    total = scattered(heads)
    g_query, g_key, g_value = (total[:, i * part : (i + 1) * part] for i in range(3))
    small = jnp.concatenate(small_total(*lax.psum((small, *others(small)), "dp")))
    return g_query, g_key, g_value, total[:, 3 * part :].T, g_expand, g_reduce.T, small


def others(small):
    near, far = (swap(small, "mp", 4, bit) for bit in range(2))
    return [near, far, swap(far, "mp", 4, 0)]


def total_of(*values):
    return sum(v.astype(F32) for v in values).astype(BF)


def arranged(result, grad_tokens, part, g_query, g_key, g_value, g_output, g_expand, g_reduce, small):
    b_reduce, b_output, gain_two, shift_two, gain_one, shift_one = (small[i] for i in range(2, 8))
    return (
        result,
        grad_tokens,
        g_query,
        small[1, :part],
        g_key,
        g_value,
        small[1, part : 2 * part],
        g_output,
        b_output,
        g_expand,
        small[0],
        g_reduce,
        b_reduce,
        gain_one,
        shift_one,
        gain_two,
        shift_two,
    )


def local(
    sizes,
    tokens,
    visible,
    w_query,
    b_query,
    w_key,
    w_value,
    b_value,
    w_output,
    b_output,
    w_expand,
    b_expand,
    w_reduce,
    b_reduce,
    gain_first,
    shift_first,
    gain_second,
    shift_second,
    cotangent,
):
    n_dp, n_mp = sizes
    part, units, (_, rows, width) = w_query.shape[1], w_expand.shape[1], tokens.shape
    core = partial(swap, axis="mp", size=n_mp, bit=0)
    across = partial(swap, axis="mp", size=n_mp, bit=1)
    over = [partial(swap, axis="dp", size=n_dp, bit=b) for b in range(n_dp.bit_length() - 1)]
    flat, tall, moved = Held((rows, width), BF), Held((width, rows), BF), shape((rows, width), BF)
    wide, rows8, rows16 = Held((rows, width), F32), Held((8, width), F32), shape((SMALL, width), F32)
    flop = 2 * rows * width * width
    block = width // n_dp
    halving = n_dp == 8 and block % 16 == 0

    third = 4 * part // 3
    direct, first, pack0, small0 = run(
        pack_body,
        (
            stacked(w_query.T, w_key.T, w_value.T, w_output, fixed=True),
            *(
                Arg([v], v.shape, fixed=True)
                for v in (
                    b_query,
                    b_value,
                    b_expand,
                    gain_first,
                    shift_first,
                    gain_second,
                    shift_second,
                    b_output,
                    b_reduce,
                )
            ),
        ),
        [
            shape((third, width), BF),
            shape((SMALL + third, width), BF),
            shape((4 * part, width), BF),
            shape((SMALL, width), BF),
        ],
        1000,
    )
    direct, first, pack1, small1 = across(direct), across(first), core(pack0), core(small0)
    n1, n1t = run(first_norm, (own(tokens), small0), (flat, tall), flop // 100)
    exp1, red1 = core(w_expand), core(w_reduce)
    n1, pack1, small1 = tie(n1, pack1, small1)
    near = run(near_attention, (held(n1), small0, pack0, small1, pack1), heads_shapes(rows, part, 2), 2 * flop, visible)
    *near, n1, direct, w_exp, w_red, cot, exp1, red1 = tie(
        *near, n1, direct, w_expand, w_reduce, cotangent, exp1, red1
    )
    relayed, direct3 = over[0](direct), core(direct)
    exp1, red1 = tie(exp1, red1)
    branch, branch_t, cross, cross_t, d_reduce, *d_hidden = run(
        branch_of,
        (own(cot), other(cot), held(w_red), held(red1)),
        (flat, tall, flat, tall, rows8, *[flat] * 4),
        flop // 100,
        visible,
    )
    branch, first, relayed = tie(branch, first, relayed)
    pack2, pack3 = (first, direct, relayed), (core(first), direct3, core(relayed))
    *pack3, branch, n1 = tie(*pack3, branch, n1)
    small2, small3 = rows_of(pack2[0], 0, SMALL), rows_of(pack3[0], 0, SMALL)
    pack2, pack3 = pieced(*pack2), pieced(*pack3)
    half, half_t = Held((rows // 2, width), BF), Held((width, rows // 2), BF)
    half_moved = shape((rows // 2, width), BF)
    *away, resid, n2, n2t, n2a, n2b = run(
        far_attention,
        (
            held(n1),
            small2,
            pack2,
            small3,
            pack3,
            held(near[5]),
            rows_of(pack0, 3 * part, part),
            rows_of(pack1, 3 * part, part),
            own(tokens),
            small0,
        ),
        [*heads_shapes(rows, part, 2), wide, flat, tall, half_moved, half_moved],
        3 * flop,
        visible,
    )
    n2a, n2b = across(n2a), across(n2b)
    grads = shape((2, width, units), BF)
    g0, g1, de_near, mlp, dn2 = run(
        near_feed,
        (
            *map(held, (n2, exp1, w_exp, red1, w_red, d_hidden[1], d_hidden[0], n2t, branch_t)),
            small1,
            small0,
        ),
        [grads, grads, rows8, wide, wide],
        12 * flop,
    )

    def cross_half(normed, first):
        gradients = [held(v, first, rows // 2) for v in (d_hidden[3], d_hidden[2])]
        return run(
            cross_feed,
            (normed, held(exp1), held(w_exp), *gradients, small1, small0),
            [half, half, half, half, half_t, half_moved],
            3 * flop,
        )

    g0, g1, n2a = tie(g0, g1, n2a)
    *half_a, dn2_back = cross_half(n2a, 0)
    got_a = across(dn2_back)
    half_a[0], n2b = tie(half_a[0], n2b)
    *half_b, dn2_back = cross_half(n2b, rows // 2)
    got_b = across(dn2_back)
    near_a, near_b = ([held(v) for v in (h[0], h[1], h[4])] for h in (half_a, half_b))
    g1, de_one = run(
        cross_one, (held(cross_t), g1, held(de_near), *near_a, *near_b), [grads, rows8], 2 * flop
    )
    g1, de_one, got_a = tie(g1, de_one, got_a)
    got0 = core(g1)
    near_a, near_b = ([held(v) for v in (h[0], h[2], h[3], h[4])] for h in (half_a, half_b))
    de_near, g1 = tie(de_near, g1)
    g0, de_zero, mlp_back = run(
        cross_zero,
        (held(cross_t), g0, *map(held, (de_near, red1, w_red)), *near_a, *near_b),
        [grads, rows8, moved],
        4 * flop,
    )
    if halving:
        g0, got0, mlp_back = tie(g0, got0, mlp_back)
    mlp_got = across(mlp_back)
    if halving:
        (pay_x, pay_z), (kept_e, kept_r), _ = stage(
            [
                ("halve", (entry(g0, 0), entry(got0, 0)), 0, 0, block),
                ("halve", (entry(g0, 1), entry(got0, 1)), 1, 1, 2 * block),
            ],
            width,
        )
        got_e, got_r = over[0](pay_x), over[1](pay_z)
        got_b, kept_e = tie(got_b, kept_e)
    grads = shape((width, 4 * part), BF)
    extra = (pltpu.VMEM((rows, 3 * part), BF), pltpu.VMEM((1, width), F32))

    def saved_of(saved, s):
        n = part // HD
        return [held(a, s * n, n) for a in saved[:5]] + [held(saved[5])]

    h2, h3, ds_far, dn1, grad_resid, attn, attn_t, sums2 = run(
        far_back,
        (
            held(resid),
            held(dn2),
            stacked(got_a, got_b),
            held(branch),
            small0,
            pack3,
            held(n1t),
            *map(held, away),
            pack2,
        ),
        [grads, grads, rows8, wide, wide, flat, tall, rows8],
        8 * flop,
        scratch=extra,
    )
    if halving:
        h2, h3, attn, mlp_got, got_e, got_r, kept_e = tie(h2, h3, attn, mlp_got, got_e, got_r, kept_e)
    got_h2 = core(h3)

    def back(column, attn, pack, saved, d_norm):
        return run(
            partial(slot_back, column),
            (held(attn), pack, held(attn_t), held(n1t), *saved_of(saved, column), held(d_norm)),
            [*[shape((width // 2, 4 * part), BF)] * 2, rows8, wide],
            4 * flop,
            scratch=extra,
        )

    h2, mlp_got = tie(h2, mlp_got)
    (result,) = run(
        result_body, (held(resid), held(mlp), mlp_got, small0), [shape((rows, width), BF)], flop // 100, visible
    )
    if halving:
        result_far, result_near = across(result), core(result)
        result, h2, got_h2, attn = tie(result, h2, got_h2, attn)
        (pay_z, pay_x, pay_h), (kept_e, kept_r, kept_h), _ = stage(
            [
                ("halve", (held(kept_e), got_e), 0, 1, block),
                ("halve", (held(kept_r), got_r), 1, 0, block),
                ("halve", (h2, got_h2), 2, 0, block),
            ],
            width,
        )
        got_z, got_x, got_h = over[1](pay_z), over[0](pay_x), over[0](pay_h)
        attn, kept_e, result_near = tie(attn, kept_e, result_near)
    *h1, ds1, dn1 = back(1, attn, pack1, near, dn1)
    if halving:
        attn, got_z, got_x, kept_e, *h1 = tie(attn, got_z, got_x, kept_e, *h1)
    got_h0 = [core(v) for v in h1]
    if halving:
        (pay_w,), (kept_e, kept_r), places_w = stage(
            [("halve", (held(kept_e), got_z), 0, 2, block), ("halve", (held(kept_r), got_x), 0, 2, block)], width
        )
        got_w = over[2](pay_w)
        attn, kept_e = tie(attn, kept_e)
    h0, strip, small = run(
        last_back,
        (
            held(attn),
            pack0,
            held(attn_t),
            held(n1t),
            *saved_of(near, 0),
            held(dn1),
            own(tokens),
            held(grad_resid),
            small0,
            *map(held, (de_zero, de_one, ds_far, ds1, d_reduce, sums2)),
        ),
        [grads, shape((rows, width), BF), rows16],
        4 * flop,
        scratch=extra,
    )
    if not halving:
        grad_tokens, result = (spread([v, core(v), across(v), core(across(v))]) for v in (strip, result))
        heads_got = across(total_of(h2, got_h2))
        sums = plain_sums(part, (g0, got0), (h0, jnp.concatenate(got_h0), heads_got), small)
        return arranged(result, grad_tokens, part, *sums)
    h0, strip, small, got_h, result_far, *got_h0 = tie(h0, strip, small, got_h, result_far, *got_h0)
    (pay_y, pay_x), (kept_h0,), _ = stage(
        [("sum", (held(kept_h), got_h), 0), ("halve", (h0, stacked(*got_h0)), 1, 0, block)], width
    )
    got_h0, heads_got = over[0](pay_x), across(pay_y)
    kept_h0, small = tie(kept_h0, small)
    small_got = others(small)
    kept_h0, strip, got_w, *small_got = tie(kept_h0, strip, got_w, *small_got)
    (small,) = run(small_body, (small, *small_got), [rows16], 1000)
    small_got = over[0](small)
    strip_far, strip_near, result_diag = across(strip), core(strip), core(result_far)
    small, kept_h0, result, result_diag = tie(small, kept_h0, result, result_diag)
    first_w, second_w = (rows_of(got_w, place[1], place[2]) for place in places_w)
    g_expand, g_reduce = run(
        feeds_body,
        (held(kept_e), first_w, held(kept_r), second_w),
        [shape((block, units), F32), shape((units, block), F32)],
        1000,
    )
    result = spread([result, result_near, result_far, result_diag])
    result, g_expand, kept_h0, got_h0, heads_got, small_got = tie(
        result, g_expand, kept_h0, got_h0, heads_got, small_got
    )
    column = n_dp // 2
    (sums,) = run(
        partial(blocks_body, block),
        (held(kept_h0), got_h0, heads_got, small, small_got),
        [shape((column * (block + SMALL), width), BF)],
        1000,
    )
    columns = [[2 * z + x for z in range(column)] for x in range(2)]
    sums_got = lax.all_to_all(sums, "dp", 0, 0, axis_index_groups=columns, tiled=True)
    sums, strip_far = tie(sums, strip_far)
    strip_diag = core(strip_far)
    sums, strip_diag = tie(sums, strip_diag)
    grad_tokens = spread([strip, strip_near, strip_far, strip_diag])
    grad_tokens, sums_got = tie(grad_tokens, sums_got)
    narrow, thin = shape((block, part), F32), shape((part, block), F32)
    *heads, small = run(partial(heads_body, part), (sums_got,), [narrow, narrow, narrow, thin, rows16], 1000)
    return arranged(result, grad_tokens, part, *heads, g_expand, g_reduce, small)


def solution(mesh):
    placed = (
        P("dp", None, None),
        P("dp"),
        P(None, "mp"),
        P("mp"),
        P(None, "mp"),
        P(None, "mp"),
        P("mp"),
        P("mp", None),
        P(),
        P(None, "mp"),
        P("mp"),
        P("mp", None),
        P(),
        P(),
        P(),
        P(),
        P(),
        P("dp", None, None),
    )
    return jax.shard_map(
        partial(local, (mesh.shape["dp"], mesh.shape["mp"])),
        mesh=mesh,
        in_specs=placed,
        out_specs=(
            P("dp", None, None),
            P("dp", None, None),
            P("dp", "mp"),
            P("mp"),
            P("dp", "mp"),
            P("dp", "mp"),
            P("mp"),
            P("mp", "dp"),
            P(),
            P("dp", "mp"),
            P("mp"),
            P("mp", "dp"),
            P(),
            P(),
            P(),
            P(),
            P(),
        ),
        check_vma=False,
    )
```
